32 devices in a mesh: comp: 4 (over y, core), dom: 8 (over z, x).
Axes of the slice: x: 2, y: 2, z: 4, core: 2. Of those that a mesh axis runs over, the one named last changes fastest.
Arguments:
- source_field: bfloat16 [4, 8, 32, 16, 128], P('comp', 'dom'), may hold values from -108 to 108, as said below
- source_block: int32 [4, 8, 12], P('comp', 'dom'), may hold values from 0 to 31
- margin: int32 [4, 8, 12, 2], P('comp', 'dom'), may hold values from 0 to 31, as said below
- remap_weight: bfloat16 [4, 8, 12, 128, 128], P('comp', 'dom'), may hold values from 0 to 0.7, as said below
- helm_coef: float32 [256, 512], P('dom', 'comp'), may hold values from 0.05 to 1
Outputs:
- solution: float32 [16, 256, 512], P(None, 'dom', 'comp')
- residual: float32 [16, 256, 512], P(None, 'dom', 'comp')
The draws below stay inside these ranges and needn't reach their ends.
Inputs may be any that keep to these rules, and one draw needn't show every extreme that they name: `source_field`: each value is a normal or uniform draw times scales that vary by field level, cell and device. `margin`: for each device and each owner, at most 4 of the device's entries name that owner and they name at most 2 distinct target rows; on every device some owner has exactly 4 entries. `remap_weight`: Nonnegative.
All inputs are finite; a program needn't handle non-finite values.
Results may differ from the reference program's by a relative error of at most 0.0003.
Values sent between devices are 32-bit elements; how exact they have to be, the bound alone decides.
No kernel may reach another device: no remote copies, remote signals or barrier semaphores. Data moves between devices by JAX's collectives and lax.ppermute only.
A program may use at most 64 MiB of HBM per device.

```python
import math
import jax
import jax.numpy as jnp
from jax import lax

ROWS = 16
B = 128
CX = 32
SB = 32
HALF = 2
PAIRS = 6
K = 12
ITERS = 2
NX = 256
NY = 512
N_COMP = 4
N_DOM = 8


def draw_source_field(key, part):
    key_base, key_rows, key_cols = jax.random.split(key, 3)
    shape = (N_COMP, N_DOM, SB, ROWS, B)
    baseline = jnp.clip(jax.random.normal(key_base, shape, jnp.float32), -4.0, 4.0)
    comp_pos = jnp.arange(N_COMP, dtype=jnp.float32) / max(N_COMP - 1, 1)
    dom_pos = jnp.arange(N_DOM, dtype=jnp.float32) / max(N_DOM - 1, 1)
    amplitude = (1.0 + comp_pos)[:, None, None, None, None] * (1.0 + 2.0 * dom_pos)[None, :, None, None, None]
    row_scale = jnp.exp(jax.random.uniform(key_rows, (ROWS,), jnp.float32, math.log(0.3), math.log(3.0)))
    col_scale = jnp.exp(jax.random.uniform(key_cols, (B,), jnp.float32, math.log(0.3), math.log(3.0)))
    values = 0.5 * baseline * amplitude * row_scale[:, None] * col_scale
    return values.astype(jnp.bfloat16)


def draw_device(subkey):
    key_slots, key_offset, key_order = jax.random.split(subkey, 3)
    slots = jax.random.permutation(key_slots, N_COMP * HALF)[:PAIRS]
    owner = slots // HALF
    offset = jax.random.randint(key_offset, (N_COMP,), 0, CX)
    stride = CX // HALF
    target_row = (offset[owner] + slots % HALF * stride) % CX
    both_owner = jnp.concatenate([owner, owner])
    both_row = jnp.concatenate([target_row, target_row])
    shuffle = jax.random.permutation(key_order, K)
    return jnp.stack([both_owner[shuffle], both_row[shuffle]], axis=-1).astype(jnp.int32)


def draw_margin(key, part):
    device_keys = jax.random.split(jax.random.fold_in(key, 17), N_COMP * N_DOM)
    drawn = jax.vmap(draw_device)(device_keys)
    return drawn.reshape(N_COMP, N_DOM, K, 2)


def draw_remap_weight(key, part):
    key_spread, key_diag = jax.random.split(jax.random.fold_in(key, 29))
    shape = (N_COMP, N_DOM, K, B, B)
    spread_part = jax.random.uniform(key_spread, shape, jnp.float32, 0.0, 2.0) * (0.6 / B)
    diagonal_part = jax.random.uniform(key_diag, shape[:-1], jnp.float32, 0.5, 1.5) * 0.4
    values = spread_part + diagonal_part[..., None] * jnp.eye(B, dtype=jnp.float32)
    return values.astype(jnp.bfloat16)


def touch_ends(values, key, low, largest):
    spot = [jax.random.randint(jax.random.fold_in(key, axis), (), 0, length) for axis, length in enumerate(values.shape)]
    widest = values.shape.index(max(values.shape))
    next_to = spot[:widest] + [(spot[widest] + 1) % values.shape[widest]] + spot[widest + 1:]
    return values.at[tuple(spot)].set(low).at[tuple(next_to)].set(largest)


def block_levels(key, shape, pieces, smallest, high):
    def one(axis_at, shards_of):
        draws = jax.random.uniform(jax.random.fold_in(jax.random.fold_in(key, 6), axis_at), (shards_of,), jnp.float32, smallest / len(pieces), high / len(pieces))
        return jnp.repeat(jnp.exp(draws), shape[axis_at] // shards_of).reshape((-1,) + (1,) * (len(shape) - axis_at - 1))

    loudness = one(*pieces[0])
    for cut in pieces[1:]:
        loudness = loudness * one(*cut)
    return loudness


def setup_inputs(seed: int = 0) -> dict:
    keys = jax.random.split(jax.random.key(seed), 6)
    source_field = draw_source_field(jax.random.fold_in(keys[5], 71), 0)
    source_block = touch_ends(jax.random.randint(keys[1], (N_COMP, N_DOM, K), 0, SB), jax.random.fold_in(keys[1], 1), 0, SB - 1).astype(jnp.int32)
    margin = draw_margin(jax.random.fold_in(keys[5], 71), 0)
    remap_weight = draw_remap_weight(jax.random.fold_in(keys[5], 71), 0)
    helm_coef = jnp.clip(jnp.exp(math.log(1.0) - 2.9957323 * jax.random.uniform(keys[4], (NX, NY), jnp.float32) ** block_levels(keys[4], (NX, NY), ((0, 8), (1, 4)), -0.2, 0.2)), 0.05, 1.0)
    return {"source_field": source_field, "source_block": source_block, "margin": margin, "remap_weight": remap_weight, "helm_coef": helm_coef}


def operate(current, helm_coef):
    padded = jnp.pad(current, ((0, 0), (1, 1), (1, 1)))
    beside = padded[:, 2:, 1:-1] + padded[:, :-2, 1:-1] + padded[:, 1:-1, 2:] + padded[:, 1:-1, :-2]
    return (4.0 + helm_coef) * current - beside


def row_dots(left, right):
    return jnp.sum(left * right, axis=(1, 2))


def reference(source_field, source_block, margin, remap_weight, helm_coef):
    start = jnp.zeros((ROWS, NX, NY), jnp.float32)

    def per_comp(target, inputs):
        sources, block_ids, margin_rows, weights = inputs
        picked = jnp.take_along_axis(sources, block_ids[:, :, None, None], axis=1).astype(jnp.float32)
        remapped = jnp.einsum("dkrs,dkts->dkrt", picked, weights.astype(jnp.float32), precision=lax.Precision.HIGHEST)
        dom_ids = jnp.arange(N_DOM, dtype=jnp.int32)[:, None, None]
        col_idx = margin_rows[:, :, 0][:, :, None] * B + jnp.arange(B, dtype=jnp.int32)[None, None, :]
        row_idx = jnp.broadcast_to(dom_ids * CX + margin_rows[:, :, 1][:, :, None], col_idx.shape)
        values = jnp.moveaxis(remapped, 2, 0)
        return target.at[:, row_idx, col_idx].add(values), None

    target, _ = lax.scan(per_comp, start, (source_field, source_block, margin, remap_weight))
    solution = jnp.zeros_like(target)
    residual = target
    direction = target
    norm_now = row_dots(residual, residual)
    for step in range(ITERS):
        applied = operate(direction, helm_coef)
        step_len = norm_now / row_dots(direction, applied)
        solution = solution + step_len[:, None, None] * direction
        residual = residual - step_len[:, None, None] * applied
        if step + 1 < ITERS:
            norm_next = row_dots(residual, residual)
            direction = residual + (norm_next / norm_now)[:, None, None] * direction
            norm_now = norm_next
    return solution, residual
```

```python
import functools
import jax
import jax.numpy as jnp
from jax import lax
from jax.experimental import pallas as pl
from jax.experimental.pallas import tpu as pltpu
from jax.sharding import PartitionSpec as P

HALF = 2
LANES = 128
LABEL = 8
HELM = 16
SHIFT = 4.0

VMEM = pl.BlockSpec(memory_space=pltpu.VMEM)
SMEM = pl.BlockSpec(memory_space=pltpu.SMEM)


def call(kernel, out_shape, in_specs, scratch=(), name=None):
    return pl.pallas_call(
        kernel,
        out_shape=out_shape,
        in_specs=in_specs,
        out_specs=jax.tree.map(lambda _: VMEM, out_shape),
        scratch_shapes=scratch,
        name=name,
        compiler_params=pltpu.CompilerParams(vmem_limit_bytes=16 * 1024 * 1024),
    )


def peer_of(me, step, devices):
    if devices & (devices - 1) == 0:
        return me ^ step, me ^ step
    return lax.rem(me + step, devices), lax.rem(me + devices - step, devices)


def lane_ids(rows):
    return lax.broadcasted_iota(jnp.int32, (rows, LANES), 1)


def pack_kernel(groups, ids, margin, sources, weights, helm, *rest):
    messages, (slots, labels) = rest[:groups], rest[groups:]
    levels = sources.shape[1]
    entries = ids.shape[0]
    slots[...] = jnp.zeros_like(slots)
    for at in range((groups + 2) * HALF):
        labels[at] = -1
    for k in range(entries):
        base = (margin[0, k] + 1) * HALF
        row = margin[1, k]
        first = labels[base]
        later = jnp.logical_and(first >= 0, first != row).astype(jnp.int32)
        labels[base + later] = row
        part = lax.dot_general(
            sources[ids[k]], weights[k], (((1,), (1,)), ((), ())), preferred_element_type=jnp.float32
        )
        slots[base + later] += part
    me = lax.axis_index("comp")
    lane = lane_ids(levels)
    lane8 = lane_ids(8)
    packed = jnp.zeros((8, LANES), jnp.float32)
    for g in range(helm.shape[0] // 8):
        at = HELM + 2 * g
        turned = pltpu.roll(helm[8 * g : 8 * g + 8, :], at + 1, 1)
        packed = jnp.where((lane8 == at) | (lane8 == at + 1), turned, packed)
    packed = jnp.concatenate([packed, jnp.zeros((levels - 8, LANES), jnp.float32)], axis=0)
    for step in range(groups):
        to, _ = peer_of(me, step, groups)
        base = (to + 1) * HALF
        out = messages[step]
        out[0] = slots[base]
        out[1] = slots[base + 1]
        left, right = base - HALF, base + HALF
        side = jnp.where(lane < 2, slots[right], packed)
        side = jnp.where(lane >= LANES - 2, slots[left], side)
        side = jnp.where((lane >= 2) & (lane < 4), pltpu.roll(slots[right + 1], 2, 1), side)
        side = jnp.where(
            (lane >= LANES - 4) & (lane < LANES - 2), pltpu.roll(slots[left + 1], LANES - 2, 1), side
        )
        for j, at in enumerate((base, base + 1, left, left + 1, right, right + 1)):
            side = jnp.where(lane == LABEL + j, labels[at].astype(jnp.float32), side)
        out[2] = side


def assemble_kernel(groups, helm, *rest):
    messages, (field, outer, helm_outer, swap_a, swap_b) = rest[:groups], rest[groups:]
    rows, levels, _ = field.shape
    me = lax.axis_index("comp")
    lane = lane_ids(levels)
    lane8 = lane_ids(8)
    blocks, tags, cols, col_tags = [], [], [], []
    for g in range(rows // 8):
        helm_outer[8 * g : 8 * g + 8, :] = jnp.zeros((8, LANES), jnp.float32)
    for step in range(groups):
        _, source = peer_of(me, step, groups)
        got = messages[step]
        side = got[2]

        def tag(j):
            return jnp.broadcast_to(side[:, LABEL + j : LABEL + j + 1], side.shape)

        blocks += [got[0], got[1]]
        tags += [tag(0), tag(1)]
        cols.append(jnp.where((lane < 2) | (lane >= LANES - 2), side, 0.0))
        col_tags.append(jnp.where(lane < LANES // 2, tag(4), tag(2)))
        inner = jnp.where(lane < LANES // 2, pltpu.roll(side, LANES - 2, 1), pltpu.roll(side, 2, 1))
        cols.append(jnp.where((lane < 2) | (lane >= LANES - 2), inner, 0.0))
        col_tags.append(jnp.where(lane < LANES // 2, tag(5), tag(3)))
        if step:
            top = side[:8]
            for g in range(rows // 8):
                turned = pltpu.roll(top, LANES - (HELM + 2 * g + 1), 1)
                mine = ((lane8 == LANES - 1) & (source == me - 1)) | ((lane8 == 0) & (source == me + 1))
                at = pl.ds(8 * g, 8)
                helm_outer[at, :] = jnp.where(mine, turned, helm_outer[at, :])

    def total(parts):
        while len(parts) > 1:
            parts = [a + b for a, b in zip(parts[::2], parts[1::2])] + parts[len(parts) // 2 * 2 :]
        return parts[0]

    for row in range(rows):
        at = float(row)
        field[row] = total([jnp.where(t == at, b, 0.0) for t, b in zip(tags, blocks)])
        outer[row] = total([jnp.where(t == at, b, 0.0) for t, b in zip(col_tags, cols)])
    even = lax.rem(lax.axis_index("dom"), 2) == 0
    for out, low in ((swap_a, jnp.logical_not(even)), (swap_b, even)):
        edge = jnp.where(low, 0, rows - 1)
        beyond = jnp.where(low, 1, rows - 2)
        out[0:levels] = field[edge]
        out[levels : 2 * levels] = field[beyond]
        out[2 * levels : 3 * levels] = outer[edge]
        out[3 * levels :] = jnp.broadcast_to(helm[pl.ds(edge, 1), :], (8, LANES))


def moments_kernel(helm, helm_outer, field, outer, got_a, got_b, image, second, partial):
    rows, levels, _ = field.shape
    comp, comps = lax.axis_index("comp"), lax.axis_size("comp")
    dom, doms = lax.axis_index("dom"), lax.axis_size("dom")
    even = lax.rem(dom, 2) == 0
    lane = lane_ids(levels)
    first, last = lane == 0, lane == LANES - 1

    def left(x, beside):
        return pltpu.roll(jnp.where(last, beside, x), 1, 1)

    def right(x, beside):
        return pltpu.roll(jnp.where(first, beside, x), LANES - 1, 1)

    def halo(at):
        a, b = got_a[at], got_b[at]
        return jnp.where(even, b, a), jnp.where(even, a, b)

    near, far = pl.ds(0, levels), pl.ds(levels, levels)
    corner, coef = pl.ds(2 * levels, levels), pl.ds(3 * levels, 1)
    above, below = halo(near)
    above2, below2 = halo(far)
    above_outer, below_outer = halo(corner)
    helm_above, helm_below = halo(coef)

    def r(i):
        return above2 if i == -2 else above if i == -1 else below if i == rows else below2 if i == rows + 1 else field[i]

    def e(i):
        return above_outer if i == -1 else below_outer if i == rows else outer[i]

    def h(i):
        return helm_above if i == -1 else helm_below if i == rows else helm[i : i + 1, :]

    def apply(i):
        x = r(i)
        return h(i) * x - ((left(x, e(i)) + right(x, e(i))) + (r(i - 1) + r(i + 1)))

    inside = (last & (comp > 0)) | (first & (comp < comps - 1))
    before = jnp.where(dom > 0, apply(-1), 0.0)
    after = jnp.where(dom < doms - 1, apply(rows), 0.0)
    for i in range(rows):
        image[i] = apply(i)
    sums = [jnp.zeros((levels, LANES), jnp.float32) for _ in range(4)]
    for i in range(rows):
        x, beside, u = field[i], outer[i], image[i]
        out = helm_outer[i : i + 1, :] * beside - ((left(beside, x) + right(beside, x)) + (e(i - 1) + e(i + 1)))
        out = jnp.where(inside, out, 0.0)
        up = before if i == 0 else image[i - 1]
        down = after if i == rows - 1 else image[i + 1]
        z = helm[i : i + 1, :] * u - ((left(u, out) + right(u, out)) + (up + down))
        second[i] = z
        for j, (a, b) in enumerate(((x, x), (x, u), (u, u), (u, z))):
            sums[j] = sums[j] + a * b
    stacked = jnp.concatenate(sums + [jnp.zeros((LANES - 4 * levels, LANES), jnp.float32)], axis=0)
    line = jnp.sum(stacked.T, axis=0, keepdims=True)
    for d in range(partial.shape[0]):
        partial[d] = line


def final_kernel(partials, field, image, second, solution, residual):
    rows, levels, _ = field.shape
    line = partials[0]
    for d in range(1, partials.shape[0]):
        line = line + partials[d]
    lane = lane_ids(levels)
    level = lax.broadcasted_iota(jnp.int32, (levels, LANES), 0)
    rr, p, q, s = [
        jnp.sum(jnp.where(lane == level + j * levels, line, 0.0), axis=1, keepdims=True) for j in range(4)
    ]
    mean = p / rr
    square = q / rr
    spread = square - mean * mean
    third = s / rr - mean * (3.0 * square - 2.0 * mean * mean)
    along = SHIFT + mean
    a0 = 1.0 / along
    beta = a0 * a0 * spread
    a1 = 1.0 / (third / spread + along - a0 * spread)
    c1 = 1.0 + beta - SHIFT * a0
    wide = lambda x: jnp.broadcast_to(x, (levels, LANES))
    sol_r, sol_u = wide(a0 + a1 * c1), wide(-a1 * a0)
    res_r = wide(1.0 - SHIFT * a0 - SHIFT * a1 * c1)
    res_u = wide(-a0 - a1 * (c1 - SHIFT * a0))
    res_y = wide(a1 * a0)
    for i in range(rows):
        x, u, y = field[i], image[i], second[i]
        at = pl.ds(i, levels, stride=rows)
        solution[at, :] = sol_r * x + sol_u * u
        residual[at, :] = (res_r * x + res_u * u) + res_y * y


def per_device(source_field, source_block, margin, remap_weight, helm):
    sources, weights = source_field[0, 0], remap_weight[0, 0]
    ids, marks = source_block[0, 0], margin[0, 0].T
    groups, doms = lax.axis_size("comp"), lax.axis_size("dom")
    levels = sources.shape[1]
    rows = helm.shape[0]
    f32 = lambda *shape: jax.ShapeDtypeStruct(shape, jnp.float32)
    messages = call(
        functools.partial(pack_kernel, groups),
        [f32(3, levels, LANES)] * groups,
        [SMEM, SMEM, VMEM, VMEM, VMEM],
        [pltpu.VMEM(((groups + 2) * HALF, levels, LANES), jnp.float32), pltpu.SMEM(((groups + 2) * HALF,), jnp.int32)],
        name="pack",
    )(ids, marks, sources, weights, helm)
    arrived = [messages[0]]
    for step in range(1, groups):
        pairs = [(c, int(peer_of(c, step, groups)[0]) if groups & (groups - 1) == 0 else (c + step) % groups) for c in range(groups)]
        arrived.append(lax.ppermute(messages[step], "comp", pairs))
    cube = f32(rows, levels, LANES)
    swap = f32(3 * levels + 8, LANES)
    field, outer, helm_outer, swap_a, swap_b = call(
        functools.partial(assemble_kernel, groups),
        [cube, cube, f32(rows, LANES), swap, swap],
        [VMEM] * (1 + groups),
        name="assemble",
    )(helm, *arrived)
    pairs_a = [(d, d ^ 1) for d in range(doms) if d ^ 1 < doms]
    pairs_b = [(d, e) for d in range(doms) for e in [((d + 1) ^ 1) - 1] if 0 <= e < doms]
    got_b = lax.ppermute(swap_b, "dom", pairs_b)
    got_a = lax.ppermute(swap_a, "dom", pairs_a)
    devices = groups * doms
    image, second, partial = call(
        moments_kernel, [cube, cube, f32(devices, 1, LANES)], [VMEM] * 6, name="moments"
    )(helm, helm_outer, field, outer, got_a, got_b)
    partials = lax.all_to_all(partial, ("comp", "dom"), split_axis=0, concat_axis=0, tiled=True)
    flat = f32(levels * rows, LANES)
    outs = call(final_kernel, [flat, flat], [VMEM] * 4, name="final")(partials, field, image, second)
    return tuple(out.reshape(levels, rows, LANES) for out in outs)


def solution(mesh):
    placed = (
        P("comp", "dom", None, None, None),
        P("comp", "dom", None),
        P("comp", "dom", None, None),
        P("comp", "dom", None, None, None),
        P("dom", "comp"),
    )
    return jax.shard_map(
        per_device,
        mesh=mesh,
        in_specs=placed,
        out_specs=(P(None, "dom", "comp"), P(None, "dom", "comp")),
        check_vma=False,
    )
```

```python
import functools
import jax
import jax.numpy as jnp
from jax import lax
from jax.experimental import pallas as pl
from jax.experimental.pallas import tpu as pltpu
from jax.sharding import PartitionSpec as P

HALF = 2
LANES = 128
LABEL = 8
HELM = 16
SHIFT = 4.0
CHUNKS = 4

VMEM = pl.BlockSpec(memory_space=pltpu.VMEM)
HBM = pl.BlockSpec(memory_space=pltpu.HBM)


def call(kernel, out_shape, in_specs, scratch=(), name=None, out_spec=VMEM, flops=0):
    return pl.pallas_call(
        kernel,
        out_shape=out_shape,
        in_specs=in_specs,
        out_specs=jax.tree.map(lambda _: out_spec, out_shape),
        scratch_shapes=scratch,
        name=name,
        compiler_params=pltpu.CompilerParams(vmem_limit_bytes=16 * 1024 * 1024),
        cost_estimate=pl.CostEstimate(flops=flops, bytes_accessed=flops // 8, transcendentals=0) if flops else None,
    )


def peer_of(me, step, devices):
    if devices & (devices - 1) == 0:
        return me ^ step, me ^ step
    return lax.rem(me + step, devices), lax.rem(me + devices - step, devices)


def lane_ids(rows):
    return lax.broadcasted_iota(jnp.int32, (rows, LANES), 1)


def left(x, beside):
    return pltpu.roll(jnp.where(lane_ids(x.shape[0]) == LANES - 1, beside, x), 1, 1)


def right(x, beside):
    return pltpu.roll(jnp.where(lane_ids(x.shape[0]) == 0, beside, x), LANES - 1, 1)


def across(h, x, beside):
    return h * x - (left(x, beside) + right(x, beside))


def total(parts):
    while len(parts) > 1:
        parts = [a + b for a, b in zip(parts[::2], parts[1::2])] + parts[len(parts) // 2 * 2 :]
    return parts[0]


def pack_kernel(groups, ids_in, margin_in, sources_in, weights_in, helm_in, *rest):
    messages = rest[:groups]
    slots, labels, ids, margin, sources, weights, helm, sems = rest[groups:]
    levels = sources.shape[1]
    entries = ids.shape[0]
    copies = [
        pltpu.make_async_copy(src, dst, sems.at[j])
        for j, (src, dst) in enumerate(((margin_in, margin), (ids_in, ids), (sources_in, sources), (helm_in, helm)))
    ]
    cuts = [entries * j // CHUNKS for j in range(CHUNKS + 1)]
    chunks = []
    for j, (lo, hi) in enumerate(zip(cuts, cuts[1:])):
        at = pl.ds(lo, hi - lo)
        chunks.append(pltpu.make_async_copy(weights_in.at[at], weights.at[at], sems.at[len(copies) + j]))
    for copy in copies[:3] + chunks + copies[3:]:
        copy.start()
    slots[...] = jnp.zeros_like(slots)
    for at in range((groups + 2) * HALF):
        labels[at] = -1
    copies[0].wait()
    places = []
    for k in range(entries):
        base = (margin[0, k] + 1) * HALF
        row = margin[1, k]
        first = labels[base]
        later = jnp.logical_and(first >= 0, first != row).astype(jnp.int32)
        labels[base + later] = row
        places.append(base + later)
    copies[1].wait()
    copies[2].wait()
    for j, (lo, hi) in enumerate(zip(cuts, cuts[1:])):
        chunks[j].wait()
        parts = [
            lax.dot_general(
                sources[ids[k]], weights[k], (((1,), (1,)), ((), ())), preferred_element_type=jnp.float32
            )
            for k in range(lo, hi)
        ]
        for k in range(lo, hi):
            slots[places[k]] += parts[k - lo]
    copies[3].wait()
    me = lax.axis_index("comp")
    lane = lane_ids(levels)
    lane8 = lane_ids(8)
    packed = jnp.zeros((8, LANES), jnp.float32)
    for g in range(helm.shape[0] // 8):
        at = HELM + 2 * g
        turned = pltpu.roll(helm[8 * g : 8 * g + 8, :], at + 1, 1)
        packed = jnp.where((lane8 == at) | (lane8 == at + 1), turned, packed)
    packed = jnp.concatenate([packed, jnp.zeros((levels - 8, LANES), jnp.float32)], axis=0)
    for step in range(groups):
        to, _ = peer_of(me, step, groups)
        base = (to + 1) * HALF
        out = messages[step]
        out[0] = slots[base]
        out[1] = slots[base + 1]
        before, after = base - HALF, base + HALF
        side = jnp.where(lane < 2, slots[after], packed)
        side = jnp.where(lane >= LANES - 2, slots[before], side)
        side = jnp.where((lane >= 2) & (lane < 4), pltpu.roll(slots[after + 1], 2, 1), side)
        side = jnp.where(
            (lane >= LANES - 4) & (lane < LANES - 2), pltpu.roll(slots[before + 1], LANES - 2, 1), side
        )
        for j, at in enumerate((base, base + 1, before, before + 1, after, after + 1)):
            side = jnp.where(lane == LABEL + j, labels[at].astype(jnp.float32), side)
        out[2] = side


def unpack(messages):
    levels = messages[0].shape[1]
    lane = lane_ids(levels)
    blocks, tags, cols, col_tags = [], [], [], []
    for got in messages:
        side = got[2]
        tag = lambda j: jnp.broadcast_to(side[:, LABEL + j : LABEL + j + 1], side.shape)
        blocks += [got[0], got[1]]
        tags += [tag(0), tag(1)]
        edge = (lane < 2) | (lane >= LANES - 2)
        inner = jnp.where(lane < LANES // 2, pltpu.roll(side, LANES - 2, 1), pltpu.roll(side, 2, 1))
        cols += [jnp.where(edge, side, 0.0), jnp.where(edge, inner, 0.0)]
        col_tags += [jnp.where(lane < LANES // 2, tag(4), tag(2)), jnp.where(lane < LANES // 2, tag(5), tag(3))]

    def cells(row):
        return total([jnp.where(t == float(row), b, 0.0) for t, b in zip(tags, blocks)])

    def beside(row):
        return total([jnp.where(t == float(row), b, 0.0) for t, b in zip(col_tags, cols)])

    return cells, beside


def edge_kernel(helm, *rest):
    messages, (swap_a, swap_b) = rest[:-2], rest[-2:]
    rows, levels = helm.shape[0], messages[0].shape[1]
    cells, beside = unpack(messages)
    lane8 = lane_ids(8)

    def message(edge, beyond):
        x, out = cells(edge), beside(edge)
        image = across(helm[edge : edge + 1, :], x, out) - cells(beyond)
        corner = out[:8]
        for g in range(1, levels // 8):
            turned = pltpu.roll(out[8 * g : 8 * g + 8], 2 * g, 1)
            corner = jnp.where((lane8 == 2 * g - 1) | (lane8 == 2 * g), turned, corner)
        return x, image, corner

    low, high = message(0, 1), message(rows - 1, rows - 2)
    even = lax.rem(lax.axis_index("dom"), 2) == 0
    at = 0
    for a, b in zip(low, high):
        to = pl.ds(at, a.shape[0])
        swap_a[to] = jnp.where(even, b, a)
        swap_b[to] = jnp.where(even, a, b)
        at += a.shape[0]


def inner_kernel(groups, helm, *rest):
    messages, (field, outer, helm_outer, image, second, sums) = rest[:groups], rest[groups:]
    rows, levels, _ = field.shape
    me, comps = lax.axis_index("comp"), lax.axis_size("comp")
    lane, lane8 = lane_ids(levels), lane_ids(8)
    for g in range(rows // 8):
        helm_outer[8 * g : 8 * g + 8, :] = jnp.zeros((8, LANES), jnp.float32)
    for step in range(1, groups):
        _, source = peer_of(me, step, groups)
        top = messages[step][2, :8, :]
        mine = ((lane8 == LANES - 1) & (source == me - 1)) | ((lane8 == 0) & (source == me + 1))
        for g in range(rows // 8):
            at = pl.ds(8 * g, 8)
            turned = pltpu.roll(top, LANES - (HELM + 2 * g + 1), 1)
            helm_outer[at, :] = jnp.where(mine, turned, helm_outer[at, :])
    cells, beside = unpack(messages)
    for i in range(rows):
        field[i] = cells(i)
        outer[i] = beside(i)
    inside = ((lane == LANES - 1) & (me > 0)) | ((lane == 0) & (me < comps - 1))
    for i in range(1, rows - 1):
        x = field[i]
        image[i] = across(helm[i : i + 1, :], x, outer[i]) - (field[i - 1] + field[i + 1])
    parts = [jnp.zeros((levels, LANES), jnp.float32) for _ in range(4)]
    for i in range(rows):
        x = field[i]
        parts[0] = parts[0] + x * x
        if 0 < i < rows - 1:
            u = image[i]
            parts[1] = parts[1] + x * u
            parts[2] = parts[2] + u * u
        if 1 < i < rows - 2:
            out = across(helm_outer[i : i + 1, :], outer[i], x) - (outer[i - 1] + outer[i + 1])
            out = jnp.where(inside, out, 0.0)
            z = across(helm[i : i + 1, :], u, out) - (image[i - 1] + image[i + 1])
            second[i] = z
            parts[3] = parts[3] + u * z
    for j in range(4):
        sums[j] = parts[j]


def rim_kernel(helm, helm_outer, field, outer, image, sums, got_a, got_b, image_rim, second_rim, partial):
    rows, levels, _ = field.shape
    comp, comps = lax.axis_index("comp"), lax.axis_size("comp")
    dom, doms = lax.axis_index("dom"), lax.axis_size("dom")
    even = lax.rem(dom, 2) == 0
    lane = lane_ids(levels)
    inside = ((lane == LANES - 1) & (comp > 0)) | ((lane == 0) & (comp < comps - 1))
    parts = [sums[j] for j in range(4)]
    for side in range(2):
        low = side == 0
        from_b = even if low else jnp.logical_not(even)
        there = dom > 0 if low else dom < doms - 1
        row = (lambda i: i) if low else (lambda i: rows - 1 - i)

        def halo(start, size):
            at = pl.ds(start, size)
            return jnp.where(there, jnp.where(from_b, got_b[at], got_a[at]), 0.0)

        next_row, next_image, corner = halo(0, levels), halo(levels, levels), halo(2 * levels, 8)
        corners = [corner] + [pltpu.roll(corner, LANES - 2 * g, 1) for g in range(1, levels // 8)]
        next_outer = jnp.concatenate(corners, axis=0)
        h = lambda i: helm[row(i) : row(i) + 1, :]
        r = lambda i: field[row(i)]
        e = lambda i: outer[row(i)]
        ho = lambda i: helm_outer[row(i) : row(i) + 1, :]
        beyond = next_image - jnp.where(there, r(0), 0.0)
        u0 = across(h(0), r(0), e(0)) - (next_row + r(1))
        u1, u2 = image[row(1)], image[row(2)]
        out0 = jnp.where(inside, across(ho(0), e(0), r(0)) - (next_outer + e(1)), 0.0)
        out1 = jnp.where(inside, across(ho(1), e(1), r(1)) - (e(0) + e(2)), 0.0)
        z0 = across(h(0), u0, out0) - (beyond + u1)
        z1 = across(h(1), u1, out1) - (u0 + u2)
        image_rim[side] = u0
        second_rim[2 * side] = z0
        second_rim[2 * side + 1] = z1
        parts[1] = parts[1] + r(0) * u0
        parts[2] = parts[2] + u0 * u0
        parts[3] = parts[3] + (u0 * z0 + u1 * z1)
    stacked = jnp.concatenate(parts + [jnp.zeros((LANES - 4 * levels, LANES), jnp.float32)], axis=0)
    line = jnp.sum(stacked.T, axis=0, keepdims=True)
    for d in range(partial.shape[0]):
        partial[d] = line


def final_kernel(partials, field, image, second, image_rim, second_rim, solution_out, residual_out, solution, residual, sems):
    rows, levels, _ = field.shape
    lines = [partials[d] for d in range(partials.shape[0])]
    line = total(lines)
    lane = lane_ids(levels)
    level = lax.broadcasted_iota(jnp.int32, (levels, LANES), 0)
    rr, p, q, s = [
        jnp.sum(jnp.where(lane == level + j * levels, line, 0.0), axis=1, keepdims=True) for j in range(4)
    ]
    mean = p / rr
    square = q / rr
    spread = square - mean * mean
    third = s / rr - mean * (3.0 * square - 2.0 * mean * mean)
    along = SHIFT + mean
    a0 = 1.0 / along
    beta = a0 * a0 * spread
    a1 = 1.0 / (third / spread + along - a0 * spread)
    c1 = 1.0 + beta - SHIFT * a0
    coefs = (
        a0 + a1 * c1,
        -a1 * a0,
        1.0 - SHIFT * a0 - SHIFT * a1 * c1,
        -a0 - a1 * (c1 - SHIFT * a0),
        a1 * a0,
    )
    copies = []
    for g in range(levels // 8):
        part = slice(8 * g, 8 * g + 8)
        sol_r, sol_u, res_r, res_u, res_z = [jnp.broadcast_to(c[part], (8, LANES)) for c in coefs]
        for i in range(rows):
            x = field[i, part, :]
            u = image_rim[0 if i == 0 else 1, part, :] if i in (0, rows - 1) else image[i, part, :]
            rim = {0: 0, 1: 1, rows - 1: 2, rows - 2: 3}.get(i)
            z = second[i, part, :] if rim is None else second_rim[rim, part, :]
            at = pl.ds(8 * g * rows + i, 8, stride=rows)
            solution[at, :] = sol_r * x + sol_u * u
            residual[at, :] = (res_r * x + res_u * u) + res_z * z
        at = pl.ds(8 * g * rows, 8 * rows)
        for j, (src, dst) in enumerate(((solution, solution_out), (residual, residual_out))):
            copies.append(pltpu.make_async_copy(src.at[at], dst.at[at], sems.at[2 * g + j]))
            copies[-1].start()
    for copy in copies:
        copy.wait()


def per_device(source_field, source_block, margin, remap_weight, helm):
    sources, weights = source_field[0, 0], remap_weight[0, 0]
    ids, marks = source_block[0, 0], margin[0, 0].T
    groups, doms = lax.axis_size("comp"), lax.axis_size("dom")
    levels = sources.shape[1]
    rows = helm.shape[0]
    f32 = lambda *shape: jax.ShapeDtypeStruct(shape, jnp.float32)
    slots = (groups + 2) * HALF
    messages = call(
        functools.partial(pack_kernel, groups),
        [f32(3, levels, LANES)] * groups,
        [HBM] * 5,
        [
            pltpu.VMEM((slots, levels, LANES), jnp.float32),
            pltpu.SMEM((slots,), jnp.int32),
            pltpu.SMEM(ids.shape, jnp.int32),
            pltpu.SMEM(marks.shape, jnp.int32),
            pltpu.VMEM(sources.shape, sources.dtype),
            pltpu.VMEM(weights.shape, weights.dtype),
            pltpu.VMEM(helm.shape, helm.dtype),
            pltpu.SemaphoreType.DMA((4 + CHUNKS,)),
        ],
        name="pack",
    )(ids, marks, sources, weights, helm)
    arrived = [messages[0]]
    for step in range(1, groups):
        if groups & (groups - 1) == 0:
            pairs = [(c, c ^ step) for c in range(groups)]
        else:
            pairs = [(c, (c + step) % groups) for c in range(groups)]
        arrived.append(lax.ppermute(messages[step], "comp", pairs))
    swap = f32(2 * levels + 8, LANES)
    swap_a, swap_b = call(edge_kernel, [swap, swap], [VMEM] * (1 + groups), name="edge")(helm, *arrived)

    def pairing(beside):
        pairs = []
        for c in range(groups):
            for d in range(doms):
                e = beside(d)
                there = (c, e) if 0 <= e < doms else (c ^ 1, d)
                if there[0] < groups:
                    pairs.append((c * doms + d, there[0] * doms + there[1]))
        return pairs

    got_a = lax.ppermute(swap_a, ("comp", "dom"), pairing(lambda d: d ^ 1))
    got_b = lax.ppermute(swap_b, ("comp", "dom"), pairing(lambda d: ((d + 1) ^ 1) - 1))
    cube, rim = f32(rows, levels, LANES), f32(2, levels, LANES)
    field, outer, helm_outer, image, second, sums = call(
        functools.partial(inner_kernel, groups),
        [cube, cube, f32(rows, LANES), cube, cube, f32(4, levels, LANES)],
        [VMEM] * (1 + groups),
        name="inner",
        flops=60 * rows * levels * LANES,
    )(helm, *arrived)
    image_rim, second_rim, partial = call(
        rim_kernel,
        [rim, f32(4, levels, LANES), f32(groups * doms, 1, LANES)],
        [VMEM] * 8,
        name="rim",
    )(helm, helm_outer, field, outer, image, sums, got_a, got_b)
    partials = lax.all_to_all(partial, ("comp", "dom"), split_axis=0, concat_axis=0, tiled=True)
    flat = f32(levels * rows, LANES)
    outs = call(
        final_kernel,
        [flat, flat],
        [VMEM] * 6,
        [pltpu.VMEM(flat.shape, flat.dtype)] * 2 + [pltpu.SemaphoreType.DMA((levels // 4,))],
        name="final",
        out_spec=HBM,
    )(partials, field, image, second, image_rim, second_rim)
    return tuple(out.reshape(levels, rows, LANES) for out in outs)


def solution(mesh):
    placed = (
        P("comp", "dom", None, None, None),
        P("comp", "dom", None),
        P("comp", "dom", None, None),
        P("comp", "dom", None, None, None),
        P("dom", "comp"),
    )
    return jax.shard_map(
        per_device,
        mesh=mesh,
        in_specs=placed,
        out_specs=(P(None, "dom", "comp"), P(None, "dom", "comp")),
        check_vma=False,
    )
```

```python
import functools
import jax
import jax.numpy as jnp
from jax import lax
from jax.experimental import pallas as pl
from jax.experimental.pallas import tpu as pltpu
from jax.sharding import PartitionSpec as P

HALF = 2
LANES = 128
LABEL = 8
HELM = 16
SHIFT = 4.0
CHUNKS = 4

VMEM = pl.BlockSpec(memory_space=pltpu.VMEM)
HBM = pl.BlockSpec(memory_space=pltpu.HBM)


def call(kernel, out_shape, in_specs, scratch=(), name=None, out_spec=VMEM, flops=0, limit=16 * 1024 * 1024):
    return pl.pallas_call(
        kernel,
        out_shape=out_shape,
        in_specs=in_specs,
        out_specs=jax.tree.map(lambda _: out_spec, out_shape),
        scratch_shapes=scratch,
        name=name,
        compiler_params=pltpu.CompilerParams(vmem_limit_bytes=limit),
        cost_estimate=pl.CostEstimate(flops=flops, bytes_accessed=flops // 8, transcendentals=0) if flops else None,
    )


def peer_of(me, step, devices):
    if devices & (devices - 1) == 0:
        return me ^ step, me ^ step
    return lax.rem(me + step, devices), lax.rem(me + devices - step, devices)


def steps_of(devices):
    return [*range(0, devices, 2), *range(1, devices, 2)]


def lane_ids(rows):
    return lax.broadcasted_iota(jnp.int32, (rows, LANES), 1)


def left(x, beside):
    return pltpu.roll(jnp.where(lane_ids(x.shape[0]) == LANES - 1, beside, x), 1, 1)


def right(x, beside):
    return pltpu.roll(jnp.where(lane_ids(x.shape[0]) == 0, beside, x), LANES - 1, 1)


def across(h, x, beside):
    return h * x - (left(x, beside) + right(x, beside))


def total(parts):
    while len(parts) > 1:
        parts = [a + b for a, b in zip(parts[::2], parts[1::2])] + parts[len(parts) // 2 * 2 :]
    return parts[0]


def pack_kernel(groups, ids_in, margin_in, sources_in, weights_in, helm_in, *rest):
    messages = rest[:groups]
    slots, labels, ids, margin, sources, weights, helm, sems = rest[groups:]
    levels = sources.shape[1]
    entries = ids.shape[0]
    copies = [
        pltpu.make_async_copy(src, dst, sems.at[j])
        for j, (src, dst) in enumerate(((margin_in, margin), (ids_in, ids), (sources_in, sources), (helm_in, helm)))
    ]
    cuts = [entries * j // CHUNKS for j in range(CHUNKS + 1)]
    chunks = []
    for j, (lo, hi) in enumerate(zip(cuts, cuts[1:])):
        at = pl.ds(lo, hi - lo)
        chunks.append(pltpu.make_async_copy(weights_in.at[at], weights.at[at], sems.at[len(copies) + j]))
    for copy in copies[:3] + chunks + copies[3:]:
        copy.start()
    slots[...] = jnp.zeros_like(slots)
    for at in range((groups + 2) * HALF):
        labels[at] = -1
    copies[0].wait()
    places = []
    for k in range(entries):
        base = (margin[0, k] + 1) * HALF
        row = margin[1, k]
        first = labels[base]
        later = jnp.logical_and(first >= 0, first != row).astype(jnp.int32)
        labels[base + later] = row
        places.append(base + later)
    copies[1].wait()
    copies[2].wait()
    for j, (lo, hi) in enumerate(zip(cuts, cuts[1:])):
        chunks[j].wait()
        parts = [
            lax.dot_general(
                sources[ids[k]], weights[k], (((1,), (1,)), ((), ())), preferred_element_type=jnp.float32
            )
            for k in range(lo, hi)
        ]
        for k in range(lo, hi):
            slots[places[k]] += parts[k - lo]
    copies[3].wait()
    me = lax.axis_index("comp")
    lane = lane_ids(levels)
    lane8 = lane_ids(8)
    packed = jnp.zeros((8, LANES), jnp.float32)
    for g in range(helm.shape[0] // 8):
        at = HELM + 2 * g
        turned = pltpu.roll(helm[8 * g : 8 * g + 8, :], at + 1, 1)
        packed = jnp.where((lane8 == at) | (lane8 == at + 1), turned, packed)
    packed = jnp.concatenate([packed, jnp.zeros((levels - 8, LANES), jnp.float32)], axis=0)
    for step, out in zip(steps_of(groups), messages):
        to, _ = peer_of(me, step, groups)
        base = (to + 1) * HALF
        out[0] = slots[base]
        out[1] = slots[base + 1]
        before, after = base - HALF, base + HALF
        side = jnp.where(lane < 2, slots[after], packed)
        side = jnp.where(lane >= LANES - 2, slots[before], side)
        side = jnp.where((lane >= 2) & (lane < 4), pltpu.roll(slots[after + 1], 2, 1), side)
        side = jnp.where(
            (lane >= LANES - 4) & (lane < LANES - 2), pltpu.roll(slots[before + 1], LANES - 2, 1), side
        )
        for j, at in enumerate((base, base + 1, before, before + 1, after, after + 1)):
            side = jnp.where(lane == LABEL + j, labels[at].astype(jnp.float32), side)
        out[2] = side


def unpack(messages):
    levels = messages[0].shape[1]
    lane = lane_ids(levels)
    blocks, tags, cols, col_tags = [], [], [], []
    for got in messages:
        side = got[2]
        tag = lambda j: jnp.broadcast_to(side[:, LABEL + j : LABEL + j + 1], side.shape)
        blocks += [got[0], got[1]]
        tags += [tag(0), tag(1)]
        edge = (lane < 2) | (lane >= LANES - 2)
        inner = jnp.where(lane < LANES // 2, pltpu.roll(side, LANES - 2, 1), pltpu.roll(side, 2, 1))
        cols += [jnp.where(edge, side, 0.0), jnp.where(edge, inner, 0.0)]
        col_tags += [jnp.where(lane < LANES // 2, tag(4), tag(2)), jnp.where(lane < LANES // 2, tag(5), tag(3))]

    def cells(row):
        return total([jnp.where(t == float(row), b, 0.0) for t, b in zip(tags, blocks)])

    def beside(row):
        return total([jnp.where(t == float(row), b, 0.0) for t, b in zip(col_tags, cols)])

    return cells, beside


def edge_kernel(helm, *rest):
    messages, (swap_b, swap_a) = rest[:-2], rest[-2:]
    rows, levels = helm.shape[0], messages[0].shape[1]
    cells, beside = unpack(messages)
    lane8 = lane_ids(8)

    def message(edge, beyond):
        x, out = cells(edge), beside(edge)
        image = across(helm[edge : edge + 1, :], x, out) - cells(beyond)
        corner = out[:8]
        for g in range(1, levels // 8):
            turned = pltpu.roll(out[8 * g : 8 * g + 8], 2 * g, 1)
            corner = jnp.where((lane8 == 2 * g - 1) | (lane8 == 2 * g), turned, corner)
        return x, image, corner

    low, high = message(0, 1), message(rows - 1, rows - 2)
    even = lax.rem(lax.axis_index("dom"), 2) == 0
    at = 0
    for a, b in zip(low, high):
        to = pl.ds(at, a.shape[0])
        swap_a[to] = jnp.where(even, b, a)
        swap_b[to] = jnp.where(even, a, b)
        at += a.shape[0]


def inner_kernel(groups, helm, *rest):
    messages, (field, outer, helm_outer, image, second, sums) = rest[:groups], rest[groups:]
    rows, levels, _ = field.shape
    me, comps = lax.axis_index("comp"), lax.axis_size("comp")
    lane, lane8 = lane_ids(levels), lane_ids(8)
    for g in range(rows // 8):
        helm_outer[8 * g : 8 * g + 8, :] = jnp.zeros((8, LANES), jnp.float32)
    for step, got in list(zip(steps_of(groups), messages))[1:]:
        _, source = peer_of(me, step, groups)
        top = got[2, :8, :]
        mine = ((lane8 == LANES - 1) & (source == me - 1)) | ((lane8 == 0) & (source == me + 1))
        for g in range(rows // 8):
            at = pl.ds(8 * g, 8)
            turned = pltpu.roll(top, LANES - (HELM + 2 * g + 1), 1)
            helm_outer[at, :] = jnp.where(mine, turned, helm_outer[at, :])
    cells, beside = unpack(messages)
    for i in range(rows):
        field[i] = cells(i)
        outer[i] = beside(i)
    inside = ((lane == LANES - 1) & (me > 0)) | ((lane == 0) & (me < comps - 1))
    for i in range(1, rows - 1):
        x = field[i]
        image[i] = across(helm[i : i + 1, :], x, outer[i]) - (field[i - 1] + field[i + 1])
    parts = [jnp.zeros((levels, LANES), jnp.float32) for _ in range(4)]
    for i in range(rows):
        x = field[i]
        parts[0] = parts[0] + x * x
        if 0 < i < rows - 1:
            u = image[i]
            parts[1] = parts[1] + x * u
            parts[2] = parts[2] + u * u
        if 1 < i < rows - 2:
            out = across(helm_outer[i : i + 1, :], outer[i], x) - (outer[i - 1] + outer[i + 1])
            out = jnp.where(inside, out, 0.0)
            z = across(helm[i : i + 1, :], u, out) - (image[i - 1] + image[i + 1])
            second[i] = z
            parts[3] = parts[3] + u * z
    for j in range(4):
        sums[j] = parts[j]


def rim_kernel(helm, helm_outer, field, outer, image, sums, got_b, got_a, image_rim, second_rim, partial):
    rows, levels, _ = field.shape
    comp, comps = lax.axis_index("comp"), lax.axis_size("comp")
    dom, doms = lax.axis_index("dom"), lax.axis_size("dom")
    even = lax.rem(dom, 2) == 0
    lane = lane_ids(levels)
    inside = ((lane == LANES - 1) & (comp > 0)) | ((lane == 0) & (comp < comps - 1))
    parts = [sums[j] for j in range(4)]
    for side in range(2):
        low = side == 0
        from_b = even if low else jnp.logical_not(even)
        there = dom > 0 if low else dom < doms - 1
        row = (lambda i: i) if low else (lambda i: rows - 1 - i)

        def halo(start, size):
            at = pl.ds(start, size)
            return jnp.where(there, jnp.where(from_b, got_b[at], got_a[at]), 0.0)

        next_row, next_image, corner = halo(0, levels), halo(levels, levels), halo(2 * levels, 8)
        corners = [corner] + [pltpu.roll(corner, LANES - 2 * g, 1) for g in range(1, levels // 8)]
        next_outer = jnp.concatenate(corners, axis=0)
        h = lambda i: helm[row(i) : row(i) + 1, :]
        r = lambda i: field[row(i)]
        e = lambda i: outer[row(i)]
        ho = lambda i: helm_outer[row(i) : row(i) + 1, :]
        beyond = next_image - jnp.where(there, r(0), 0.0)
        u0 = across(h(0), r(0), e(0)) - (next_row + r(1))
        u1, u2 = image[row(1)], image[row(2)]
        out0 = jnp.where(inside, across(ho(0), e(0), r(0)) - (next_outer + e(1)), 0.0)
        out1 = jnp.where(inside, across(ho(1), e(1), r(1)) - (e(0) + e(2)), 0.0)
        z0 = across(h(0), u0, out0) - (beyond + u1)
        z1 = across(h(1), u1, out1) - (u0 + u2)
        image_rim[side] = u0
        second_rim[2 * side] = z0
        second_rim[2 * side + 1] = z1
        parts[1] = parts[1] + r(0) * u0
        parts[2] = parts[2] + u0 * u0
        parts[3] = parts[3] + (u0 * z0 + u1 * z1)
    stacked = jnp.concatenate(parts + [jnp.zeros((LANES - 4 * levels, LANES), jnp.float32)], axis=0)
    line = jnp.sum(stacked.T, axis=0, keepdims=True)
    for d in range(partial.shape[0]):
        partial[d] = line


def final_kernel(partials, field, image, second, image_rim, second_rim, solution_out, residual_out, solution, residual, sems):
    rows, levels, _ = field.shape
    lines = [partials[d] for d in range(partials.shape[0])]
    line = total(lines)
    lane = lane_ids(levels)
    level = lax.broadcasted_iota(jnp.int32, (levels, LANES), 0)
    rr, p, q, s = [
        jnp.sum(jnp.where(lane == level + j * levels, line, 0.0), axis=1, keepdims=True) for j in range(4)
    ]
    mean = p / rr
    square = q / rr
    spread = square - mean * mean
    third = s / rr - mean * (3.0 * square - 2.0 * mean * mean)
    along = SHIFT + mean
    a0 = 1.0 / along
    beta = a0 * a0 * spread
    a1 = 1.0 / (third / spread + along - a0 * spread)
    c1 = 1.0 + beta - SHIFT * a0
    coefs = (
        a0 + a1 * c1,
        -a1 * a0,
        1.0 - SHIFT * a0 - SHIFT * a1 * c1,
        -a0 - a1 * (c1 - SHIFT * a0),
        a1 * a0,
    )
    copies = []
    for g in range(levels // 8):
        part = slice(8 * g, 8 * g + 8)
        sol_r, sol_u, res_r, res_u, res_z = [jnp.broadcast_to(c[part], (8, LANES)) for c in coefs]
        for i in range(rows):
            x = field[i, part, :]
            u = image_rim[0 if i == 0 else 1, part, :] if i in (0, rows - 1) else image[i, part, :]
            rim = {0: 0, 1: 1, rows - 1: 2, rows - 2: 3}.get(i)
            z = second[i, part, :] if rim is None else second_rim[rim, part, :]
            at = pl.ds(8 * g * rows + i, 8, stride=rows)
            solution[at, :] = sol_r * x + sol_u * u
            residual[at, :] = (res_r * x + res_u * u) + res_z * z
        at = pl.ds(8 * g * rows, 8 * rows)
        for j, (src, dst) in enumerate(((solution, solution_out), (residual, residual_out))):
            copies.append(pltpu.make_async_copy(src.at[at], dst.at[at], sems.at[2 * g + j]))
            copies[-1].start()
    for copy in copies:
        copy.wait()


def per_device(source_field, source_block, margin, remap_weight, helm):
    sources, weights = source_field[0, 0], remap_weight[0, 0]
    ids, marks = source_block[0, 0], margin[0, 0].T
    groups, doms = lax.axis_size("comp"), lax.axis_size("dom")
    levels = sources.shape[1]
    rows = helm.shape[0]
    f32 = lambda *shape: jax.ShapeDtypeStruct(shape, jnp.float32)
    slots = (groups + 2) * HALF
    messages = call(
        functools.partial(pack_kernel, groups),
        [f32(3, levels, LANES)] * groups,
        [HBM] * 5,
        [
            pltpu.VMEM((slots, levels, LANES), jnp.float32),
            pltpu.SMEM((slots,), jnp.int32),
            pltpu.SMEM(ids.shape, jnp.int32),
            pltpu.SMEM(marks.shape, jnp.int32),
            pltpu.VMEM(sources.shape, sources.dtype),
            pltpu.VMEM(weights.shape, weights.dtype),
            pltpu.VMEM(helm.shape, helm.dtype),
            pltpu.SemaphoreType.DMA((4 + CHUNKS,)),
        ],
        name="pack",
    )(*[pltpu.with_memory_space_constraint(x, pltpu.HBM) for x in (ids, marks, sources, weights, helm)])
    arrived = [messages[0]]
    for step, message in list(zip(steps_of(groups), messages))[1:]:
        if groups & (groups - 1) == 0:
            pairs = [(c, c ^ step) for c in range(groups)]
        else:
            pairs = [(c, (c + step) % groups) for c in range(groups)]
        arrived.append(lax.ppermute(message, "comp", pairs))
    swap = f32(2 * levels + 8, LANES)
    swap_b, swap_a = call(edge_kernel, [swap, swap], [VMEM] * (1 + groups), name="edge")(helm, *arrived)

    def pairing(beside):
        pairs = []
        for c in range(groups):
            for d in range(doms):
                e = beside(d)
                there = (c, e) if 0 <= e < doms else (c ^ 1, d)
                if there[0] < groups:
                    pairs.append((c * doms + d, there[0] * doms + there[1]))
        return pairs

    got_b = lax.ppermute(swap_b, ("comp", "dom"), pairing(lambda d: ((d + 1) ^ 1) - 1))
    got_a = lax.ppermute(swap_a, ("comp", "dom"), pairing(lambda d: d ^ 1))
    cube, rim = f32(rows, levels, LANES), f32(2, levels, LANES)
    field, outer, helm_outer, image, second, sums = call(
        functools.partial(inner_kernel, groups),
        [cube, cube, f32(rows, LANES), cube, cube, f32(4, levels, LANES)],
        [VMEM] * (1 + groups),
        name="inner",
        flops=60 * rows * levels * LANES,
    )(helm, *arrived)
    image_rim, second_rim, partial = call(
        rim_kernel,
        [rim, f32(4, levels, LANES), f32(groups * doms, 1, LANES)],
        [VMEM] * 8,
        name="rim",
    )(helm, helm_outer, field, outer, image, sums, got_b, got_a)
    partials = lax.all_to_all(partial, ("comp", "dom"), split_axis=0, concat_axis=0, tiled=True)
    flat = f32(levels * rows, LANES)
    outs = call(
        final_kernel,
        [flat, flat],
        [VMEM] * 6,
        [pltpu.VMEM(flat.shape, flat.dtype)] * 2 + [pltpu.SemaphoreType.DMA((levels // 4,))],
        name="final",
        out_spec=HBM,
    )(partials, field, image, second, image_rim, second_rim)
    return tuple(out.reshape(levels, rows, LANES) for out in outs)


def solution(mesh):
    placed = (
        P("comp", "dom", None, None, None),
        P("comp", "dom", None),
        P("comp", "dom", None, None),
        P("comp", "dom", None, None, None),
        P("dom", "comp"),
    )
    return jax.shard_map(
        per_device,
        mesh=mesh,
        in_specs=placed,
        out_specs=(P(None, "dom", "comp"), P(None, "dom", "comp")),
        check_vma=False,
    )
```

```python
import functools
import jax
import jax.numpy as jnp
from jax import lax
from jax.experimental import pallas as pl
from jax.experimental.pallas import tpu as pltpu
from jax.sharding import PartitionSpec as P

HALF = 2
LANES = 128
LABEL = 8
HELM = 16
SHIFT = 4.0
PART = 4
CHUNKS = 1

VMEM = pl.BlockSpec(memory_space=pltpu.VMEM)
HBM = pl.BlockSpec(memory_space=pltpu.HBM)


def call(kernel, out_shape, in_specs, scratch=(), name=None, out_spec=VMEM, flops=0, aliases={}):
    return pl.pallas_call(
        kernel,
        out_shape=out_shape,
        in_specs=in_specs,
        out_specs=jax.tree.map(lambda _: out_spec, out_shape),
        scratch_shapes=scratch,
        input_output_aliases=aliases,
        name=name,
        compiler_params=pltpu.CompilerParams(vmem_limit_bytes=16 * 1024 * 1024),
        cost_estimate=pl.CostEstimate(flops=flops, bytes_accessed=flops // 8, transcendentals=0) if flops else None,
    )


def peer_of(me, step, devices):
    if devices & (devices - 1) == 0:
        return me ^ step, me ^ step
    return lax.rem(me + step, devices), lax.rem(me + devices - step, devices)


def steps_of(devices):
    return [*range(0, devices, 2), *range(1, devices, 2)]


def lane_ids(rows):
    return lax.broadcasted_iota(jnp.int32, (rows, LANES), 1)


def left(x, beside):
    return pltpu.roll(jnp.where(lane_ids(x.shape[0]) == LANES - 1, beside, x), 1, 1)


def right(x, beside):
    return pltpu.roll(jnp.where(lane_ids(x.shape[0]) == 0, beside, x), LANES - 1, 1)


def across(h, x, beside):
    return h * x - (left(x, beside) + right(x, beside))


def total(parts):
    while len(parts) > 1:
        parts = [a + b for a, b in zip(parts[::2], parts[1::2])] + parts[len(parts) // 2 * 2 :]
    return parts[0]


def pack_kernel(groups, ids_in, margin_in, sources_in, weights_in, helm_in, *rest):
    messages = rest[:groups]
    slots, labels, ids, margin, sources, weights, helm, sems = rest[groups:]
    levels = sources.shape[1]
    entries = ids.shape[0]
    copies = [
        pltpu.make_async_copy(src, dst, sems.at[j])
        for j, (src, dst) in enumerate(((margin_in, margin), (ids_in, ids), (sources_in, sources), (helm_in, helm)))
    ]
    cuts = [entries * j // CHUNKS for j in range(CHUNKS + 1)]
    chunks = []
    for j, (lo, hi) in enumerate(zip(cuts, cuts[1:])):
        at = pl.ds(lo, hi - lo)
        chunks.append(pltpu.make_async_copy(weights_in.at[at], weights.at[at], sems.at[len(copies) + j]))
    for copy in copies[:2] + chunks + copies[2:]:
        copy.start()
    slots[...] = jnp.zeros_like(slots)
    for at in range((groups + 2) * HALF):
        labels[at] = -1
    me = lax.axis_index("comp")
    lane = lane_ids(levels)
    lane8 = lane_ids(8)
    bases = [(peer_of(me, step, groups)[0] + 1) * HALF for step in steps_of(groups)]
    copies[0].wait()
    places = []
    for k in range(entries):
        base = (margin[0, k] + 1) * HALF
        row = margin[1, k]
        first = labels[base]
        later = jnp.logical_and(first >= 0, first != row).astype(jnp.int32)
        labels[base + later] = row
        places.append(base + later)
    copies[3].wait()
    packed = jnp.zeros((8, LANES), jnp.float32)
    for g in range(helm.shape[0] // 8):
        at = HELM + 2 * g
        turned = pltpu.roll(helm[8 * g : 8 * g + 8, :], at + 1, 1)
        packed = jnp.where((lane8 == at) | (lane8 == at + 1), turned, packed)
    packed = jnp.concatenate([packed, jnp.zeros((levels - 8, LANES), jnp.float32)], axis=0)
    for base, out in zip(bases, messages):
        side = packed
        for j in range(3 * HALF):
            at = base + (j % HALF) + (0, -HALF, HALF)[j // HALF]
            side = jnp.where(lane == LABEL + j, labels[at].astype(jnp.float32), side)
        out[2] = side
    copies[1].wait()
    copies[2].wait()
    for chunk in chunks:
        chunk.wait()
    parts = [
        lax.dot_general(sources[ids[k]], weights[k], (((1,), (1,)), ((), ())), preferred_element_type=jnp.float32)
        for k in range(entries)
    ]
    for k in range(entries):
        slots[places[k]] += parts[k]
    for base, out in zip(bases, messages):
        out[0] = slots[base]
        out[1] = slots[base + 1]
        before, after = base - HALF, base + HALF
        side = jnp.where(lane < 2, slots[after], out[2])
        side = jnp.where(lane >= LANES - 2, slots[before], side)
        side = jnp.where((lane >= 2) & (lane < 4), pltpu.roll(slots[after + 1], 2, 1), side)
        out[2] = jnp.where(
            (lane >= LANES - 4) & (lane < LANES - 2), pltpu.roll(slots[before + 1], LANES - 2, 1), side
        )


def unpack(messages):
    levels = messages[0].shape[1]
    lane = lane_ids(levels)
    blocks, tags, cols, col_tags = [], [], [], []
    for got in messages:
        side = got[2]
        tag = lambda j: jnp.broadcast_to(side[:, LABEL + j : LABEL + j + 1], side.shape)
        blocks += [got[0], got[1]]
        tags += [tag(0), tag(1)]
        edge = (lane < 2) | (lane >= LANES - 2)
        inner = jnp.where(lane < LANES // 2, pltpu.roll(side, LANES - 2, 1), pltpu.roll(side, 2, 1))
        cols += [jnp.where(edge, side, 0.0), jnp.where(edge, inner, 0.0)]
        col_tags += [jnp.where(lane < LANES // 2, tag(4), tag(2)), jnp.where(lane < LANES // 2, tag(5), tag(3))]

    def cells(row):
        return total([jnp.where(t == float(row), b, 0.0) for t, b in zip(tags, blocks)])

    def beside(row):
        return total([jnp.where(t == float(row), b, 0.0) for t, b in zip(col_tags, cols)])

    return cells, beside


def edge_kernel(helm, *rest):
    messages, (swap_b, swap_a) = rest[:-2], rest[-2:]
    rows, levels = helm.shape[0], messages[0].shape[1]
    cells, beside = unpack(messages)
    lane8 = lane_ids(8)

    def message(edge, beyond):
        x, out = cells(edge), beside(edge)
        image = across(helm[edge : edge + 1, :], x, out) - cells(beyond)
        corner = out[:8]
        for g in range(1, levels // 8):
            turned = pltpu.roll(out[8 * g : 8 * g + 8], 2 * g, 1)
            corner = jnp.where((lane8 == 2 * g - 1) | (lane8 == 2 * g), turned, corner)
        return x, image, corner

    low, high = message(0, 1), message(rows - 1, rows - 2)
    even = lax.rem(lax.axis_index("dom"), 2) == 0
    at = 0
    for a, b in zip(low, high):
        to = pl.ds(at, a.shape[0])
        swap_a[to] = jnp.where(even, b, a)
        swap_b[to] = jnp.where(even, a, b)
        at += a.shape[0]


def inner_kernel(groups, helm, *rest):
    messages, (field, outer, helm_outer, image, second, sums) = rest[:groups], rest[groups:]
    rows, levels, _ = field.shape
    me, comps = lax.axis_index("comp"), lax.axis_size("comp")
    lane, lane8 = lane_ids(levels), lane_ids(8)
    for g in range(rows // 8):
        helm_outer[8 * g : 8 * g + 8, :] = jnp.zeros((8, LANES), jnp.float32)
    for step, got in list(zip(steps_of(groups), messages))[1:]:
        _, source = peer_of(me, step, groups)
        top = got[2, :8, :]
        mine = ((lane8 == LANES - 1) & (source == me - 1)) | ((lane8 == 0) & (source == me + 1))
        for g in range(rows // 8):
            at = pl.ds(8 * g, 8)
            turned = pltpu.roll(top, LANES - (HELM + 2 * g + 1), 1)
            helm_outer[at, :] = jnp.where(mine, turned, helm_outer[at, :])
    cells, beside = unpack(messages)
    for i in range(rows):
        field[i] = cells(i)
        outer[i] = beside(i)
    inside = ((lane == LANES - 1) & (me > 0)) | ((lane == 0) & (me < comps - 1))
    for i in range(1, rows - 1):
        x = field[i]
        image[i] = across(helm[i : i + 1, :], x, outer[i]) - (field[i - 1] + field[i + 1])
    parts = [jnp.zeros((levels, LANES), jnp.float32) for _ in range(4)]
    for i in range(rows):
        x = field[i]
        parts[0] = parts[0] + x * x
        if 0 < i < rows - 1:
            u = image[i]
            parts[1] = parts[1] + x * u
            parts[2] = parts[2] + u * u
        if 1 < i < rows - 2:
            out = across(helm_outer[i : i + 1, :], outer[i], x) - (outer[i - 1] + outer[i + 1])
            out = jnp.where(inside, out, 0.0)
            z = across(helm[i : i + 1, :], u, out) - (image[i - 1] + image[i + 1])
            second[i] = z
            parts[3] = parts[3] + u * z
    for j in range(4):
        sums[j] = parts[j]


def rim_kernel(helm, helm_outer, field, outer, image_in, second_in, sums, got_b, got_a, image, second, partial):
    rows, levels, _ = field.shape
    comp, comps = lax.axis_index("comp"), lax.axis_size("comp")
    dom, doms = lax.axis_index("dom"), lax.axis_size("dom")
    even = lax.rem(dom, 2) == 0
    lane = lane_ids(levels)
    inside = ((lane == LANES - 1) & (comp > 0)) | ((lane == 0) & (comp < comps - 1))
    parts = [sums[j] for j in range(4)]
    for side in range(2):
        low = side == 0
        from_b = even if low else jnp.logical_not(even)
        there = dom > 0 if low else dom < doms - 1
        row = (lambda i: i) if low else (lambda i: rows - 1 - i)

        def halo(start, size):
            at = pl.ds(start, size)
            return jnp.where(there, jnp.where(from_b, got_b[at], got_a[at]), 0.0)

        next_row, next_image, corner = halo(0, levels), halo(levels, levels), halo(2 * levels, 8)
        corners = [corner] + [pltpu.roll(corner, LANES - 2 * g, 1) for g in range(1, levels // 8)]
        next_outer = jnp.concatenate(corners, axis=0)
        h = lambda i: helm[row(i) : row(i) + 1, :]
        r = lambda i: field[row(i)]
        e = lambda i: outer[row(i)]
        ho = lambda i: helm_outer[row(i) : row(i) + 1, :]
        beyond = next_image - jnp.where(there, r(0), 0.0)
        u0 = across(h(0), r(0), e(0)) - (next_row + r(1))
        u1, u2 = image[row(1)], image[row(2)]
        out0 = jnp.where(inside, across(ho(0), e(0), r(0)) - (next_outer + e(1)), 0.0)
        out1 = jnp.where(inside, across(ho(1), e(1), r(1)) - (e(0) + e(2)), 0.0)
        z0 = across(h(0), u0, out0) - (beyond + u1)
        z1 = across(h(1), u1, out1) - (u0 + u2)
        image[row(0)] = u0
        second[row(0)] = z0
        second[row(1)] = z1
        parts[1] = parts[1] + r(0) * u0
        parts[2] = parts[2] + u0 * u0
        parts[3] = parts[3] + (u0 * z0 + u1 * z1)
    stacked = jnp.concatenate(parts + [jnp.zeros((LANES - 4 * levels, LANES), jnp.float32)], axis=0)
    line = jnp.sum(stacked.T, axis=0, keepdims=True)
    for d in range(partial.shape[0]):
        partial[d] = line


def final_kernel(partials, field, image, second, solution_out, residual_out, solution, residual, sems):
    levels, rows = residual_out.shape[0], residual_out.shape[1]
    line = total([partials[d] for d in range(partials.shape[0])])
    lane = lane_ids(levels)
    level = lax.broadcasted_iota(jnp.int32, (levels, LANES), 0)
    rr, p, q, s = [
        jnp.sum(jnp.where(lane == level + j * levels, line, 0.0), axis=1, keepdims=True) for j in range(4)
    ]
    mean = p / rr
    square = q / rr
    spread = square - mean * mean
    third = s / rr - mean * (3.0 * square - 2.0 * mean * mean)
    along = SHIFT + mean
    a0 = 1.0 / along
    beta = a0 * a0 * spread
    a1 = 1.0 / (third / spread + along - a0 * spread)
    c1 = 1.0 + beta - SHIFT * a0
    coefs = (
        a0 + a1 * c1,
        -a1 * a0,
        1.0 - SHIFT * a0 - SHIFT * a1 * c1,
        -a0 - a1 * (c1 - SHIFT * a0),
        a1 * a0,
    )
    coefs = [jnp.broadcast_to(c, (levels, LANES)) for c in coefs]
    copies = []
    for n in range(levels):
        sol_r, sol_u, res_r, res_u, res_z = [jnp.broadcast_to(c[n : n + 1], (8, LANES)) for c in coefs]
        for g in range(rows // 8):
            at = pl.ds(8 * g * levels + n, 8, stride=levels)
            x, u, z = field[at, :], image[at, :], second[at, :]
            to = pl.ds(8 * g, 8)
            solution[n, to, :] = sol_r * x + sol_u * u
            residual[n, to, :] = (res_r * x + res_u * u) + res_z * z
        if (n + 1) % PART == 0:
            at = pl.ds(n + 1 - PART, PART)
            for src, dst in ((solution, solution_out), (residual, residual_out)):
                copies.append(pltpu.make_async_copy(src.at[at], dst.at[at], sems.at[len(copies)]))
                copies[-1].start()
    for copy in copies:
        copy.wait()


def per_device(source_field, source_block, margin, remap_weight, helm):
    sources, weights = source_field[0, 0], remap_weight[0, 0]
    ids, marks = source_block[0, 0], margin[0, 0].T
    groups, doms = lax.axis_size("comp"), lax.axis_size("dom")
    levels = sources.shape[1]
    rows = helm.shape[0]
    f32 = lambda *shape: jax.ShapeDtypeStruct(shape, jnp.float32)
    slots = (groups + 2) * HALF
    messages = call(
        functools.partial(pack_kernel, groups),
        [f32(3, levels, LANES)] * groups,
        [HBM] * 5,
        [
            pltpu.VMEM((slots, levels, LANES), jnp.float32),
            pltpu.SMEM((slots,), jnp.int32),
            pltpu.SMEM(ids.shape, jnp.int32),
            pltpu.SMEM(marks.shape, jnp.int32),
            pltpu.VMEM(sources.shape, sources.dtype),
            pltpu.VMEM(weights.shape, weights.dtype),
            pltpu.VMEM(helm.shape, helm.dtype),
            pltpu.SemaphoreType.DMA((4 + CHUNKS,)),
        ],
        name="pack",
    )(*[pltpu.with_memory_space_constraint(x, pltpu.HBM) for x in (ids, marks, sources, weights, helm)])
    arrived = [messages[0]]
    for step, message in list(zip(steps_of(groups), messages))[1:]:
        if groups & (groups - 1) == 0:
            pairs = [(c, c ^ step) for c in range(groups)]
        else:
            pairs = [(c, (c + step) % groups) for c in range(groups)]
        arrived.append(lax.ppermute(message, "comp", pairs))
    swap = f32(2 * levels + 8, LANES)
    swap_b, swap_a = call(edge_kernel, [swap, swap], [VMEM] * (1 + groups), name="edge")(helm, *arrived)

    def pairing(beside):
        pairs = []
        for c in range(groups):
            for d in range(doms):
                e = beside(d)
                there = (c, e) if 0 <= e < doms else (c ^ 1, d)
                if there[0] < groups:
                    pairs.append((c * doms + d, there[0] * doms + there[1]))
        return pairs

    got_b = lax.ppermute(swap_b, ("comp", "dom"), pairing(lambda d: ((d + 1) ^ 1) - 1))
    got_a = lax.ppermute(swap_a, ("comp", "dom"), pairing(lambda d: d ^ 1))
    cube = f32(rows, levels, LANES)
    field, outer, helm_outer, image, second, sums = call(
        functools.partial(inner_kernel, groups),
        [cube, cube, f32(rows, LANES), cube, cube, f32(4, levels, LANES)],
        [VMEM] * (1 + groups),
        name="inner",
        flops=60 * rows * levels * LANES,
    )(helm, *arrived)
    image, second, partial = call(
        rim_kernel,
        [cube, cube, f32(groups * doms, 1, LANES)],
        [VMEM] * 9,
        name="rim",
        aliases={4: 0, 5: 1},
    )(helm, helm_outer, field, outer, image, second, sums, got_b, got_a)
    partials = lax.all_to_all(partial, ("comp", "dom"), split_axis=0, concat_axis=0, tiled=True)
    whole = f32(levels, rows, LANES)
    flat = lambda x: x.reshape(rows * levels, LANES)
    return tuple(
        call(
            final_kernel,
            [whole, whole],
            [VMEM] * 4,
            [pltpu.VMEM(whole.shape, whole.dtype)] * 2 + [pltpu.SemaphoreType.DMA((2 * levels // PART,))],
            name="final",
            out_spec=HBM,
        )(partials, flat(field), flat(image), flat(second))
    )


def solution(mesh):
    placed = (
        P("comp", "dom", None, None, None),
        P("comp", "dom", None),
        P("comp", "dom", None, None),
        P("comp", "dom", None, None, None),
        P("dom", "comp"),
    )
    return jax.shard_map(
        per_device,
        mesh=mesh,
        in_specs=placed,
        out_specs=(P(None, "dom", "comp"), P(None, "dom", "comp")),
        check_vma=False,
    )
```

```python
import functools
import jax
import jax.numpy as jnp
from jax import lax
from jax.experimental import pallas as pl
from jax.experimental.pallas import tpu as pltpu
from jax.sharding import PartitionSpec as P

HALF = 2
LANES = 128
LABEL = 8
APART = 32
HELM = 16
SHIFT = 4.0
PART = 4
PAD = 8
CHUNKS = 1

VMEM = pl.BlockSpec(memory_space=pltpu.VMEM)
HBM = pl.BlockSpec(memory_space=pltpu.HBM)


def call(kernel, out_shape, in_specs, scratch=(), name=None, out_spec=VMEM, flops=0, aliases={}):
    return pl.pallas_call(
        kernel,
        out_shape=out_shape,
        in_specs=in_specs,
        out_specs=jax.tree.map(lambda _: out_spec, out_shape),
        scratch_shapes=scratch,
        input_output_aliases=aliases,
        name=name,
        compiler_params=pltpu.CompilerParams(vmem_limit_bytes=16 * 1024 * 1024),
        cost_estimate=pl.CostEstimate(flops=flops, bytes_accessed=flops // 8, transcendentals=0) if flops else None,
    )


def peer_of(me, step, devices):
    if devices & (devices - 1) == 0:
        return me ^ step, me ^ step
    return lax.rem(me + step, devices), lax.rem(me + devices - step, devices)


def steps_of(devices):
    return [*range(0, devices, 2), *range(1, devices, 2)]


def lane_ids(rows):
    return lax.broadcasted_iota(jnp.int32, (rows, LANES), 1)


def left(x, beside):
    return pltpu.roll(jnp.where(lane_ids(x.shape[0]) == LANES - 1, beside, x), 1, 1)


def right(x, beside):
    return pltpu.roll(jnp.where(lane_ids(x.shape[0]) == 0, beside, x), LANES - 1, 1)


def across(h, x, beside):
    return h * x - (left(x, beside) + right(x, beside))


def total(parts):
    while len(parts) > 1:
        parts = [a + b for a, b in zip(parts[::2], parts[1::2])] + parts[len(parts) // 2 * 2 :]
    return parts[0]


def pack_kernel(groups, ids_in, margin_in, sources_in, weights_in, helm_in, *rest):
    messages = rest[:groups]
    slots, labels, ids, margin, sources, weights, helm, sems = rest[groups:]
    levels = sources.shape[1]
    entries = ids.shape[0]
    copies = [
        pltpu.make_async_copy(src, dst, sems.at[j])
        for j, (src, dst) in enumerate(((margin_in, margin), (ids_in, ids), (sources_in, sources), (helm_in, helm)))
    ]
    cuts = [entries * j // CHUNKS for j in range(CHUNKS + 1)]
    chunks = []
    for j, (lo, hi) in enumerate(zip(cuts, cuts[1:])):
        at = pl.ds(lo, hi - lo)
        chunks.append(pltpu.make_async_copy(weights_in.at[at], weights.at[at], sems.at[len(copies) + j]))
    for copy in copies[:2] + chunks + copies[2:]:
        copy.start()
    slots[...] = jnp.zeros_like(slots)
    for at in range((groups + 2) * HALF):
        labels[at] = -1
    me = lax.axis_index("comp")
    lane = lane_ids(levels)
    lane8 = lane_ids(8)
    bases = [(peer_of(me, step, groups)[0] + 1) * HALF for step in steps_of(groups)]
    copies[0].wait()
    places = []
    for k in range(entries):
        base = (margin[0, k] + 1) * HALF
        row = margin[1, k]
        first = labels[base]
        later = jnp.logical_and(first >= 0, first != row).astype(jnp.int32)
        labels[base + later] = row
        places.append(base + later)
    copies[3].wait()
    packed = jnp.zeros((8, LANES), jnp.float32)
    for g in range(helm.shape[0] // 8):
        at = HELM + 2 * g
        turned = pltpu.roll(helm[8 * g : 8 * g + 8, :], at + 1, 1)
        packed = jnp.where((lane8 == at) | (lane8 == at + 1), turned, packed)
    for base, out in zip(bases, messages):
        side = packed
        for j in range(3 * HALF):
            at = base + (j % HALF) + (0, -HALF, HALF)[j // HALF]
            side = jnp.where(lane8 == LABEL + j, labels[at].astype(jnp.float32), side)
        out[HALF * levels :] = side
    copies[1].wait()
    copies[2].wait()
    for chunk in chunks:
        chunk.wait()
    parts = [
        lax.dot_general(sources[ids[k]], weights[k], (((1,), (1,)), ((), ())), preferred_element_type=jnp.float32)
        for k in range(entries)
    ]
    for k in range(entries):
        slots[places[k]] += parts[k]
    for base, out in zip(bases, messages):
        out[0:levels] = slots[base]
        out[levels : 2 * levels] = slots[base + 1]
        before, after = base - HALF, base + HALF
        cols = jnp.where(lane < LANES // 2, slots[after], slots[before])
        inner = jnp.where(
            lane < LANES // 2, pltpu.roll(slots[after + 1], 2, 1), pltpu.roll(slots[before + 1], LANES - 2, 1)
        )
        cols = jnp.where((lane < 2) | (lane >= LANES - 2), cols, inner)
        side = out[HALF * levels :]
        for g in range(levels // 8):
            turned = cols[8 * g : 8 * g + 8]
            if g:
                turned = pltpu.roll(turned, APART * g, 1)
            here = (lane8 + (LANES - APART * g + 4)) % LANES < 8
            side = jnp.where(here, turned, side)
        out[HALF * levels :] = side


def side_of(message, levels):
    side = message[HALF * levels :]
    turned = [side] + [pltpu.roll(side, LANES - APART * g, 1) for g in range(1, levels // 8)]
    return side, jnp.concatenate(turned, axis=0)


def unpack(messages, levels):
    lane = lane_ids(levels)
    blocks, tags, cols, col_tags = [], [], [], []
    for got in messages:
        side, ends = side_of(got, levels)
        tag = lambda j: jnp.broadcast_to(side[0:1, LABEL + j : LABEL + j + 1], (levels, LANES))
        blocks += [got[0:levels], got[levels : 2 * levels]]
        tags += [tag(0), tag(1)]
        inner = jnp.where(lane < LANES // 2, pltpu.roll(ends, LANES - 2, 1), pltpu.roll(ends, 2, 1))
        cols += [ends, inner]
        col_tags += [jnp.where(lane < LANES // 2, tag(4), tag(2)), jnp.where(lane < LANES // 2, tag(5), tag(3))]

    def cells(row):
        return total([jnp.where(t == float(row), b, 0.0) for t, b in zip(tags, blocks)])

    def beside(row):
        return total([jnp.where(t == float(row), b, 0.0) for t, b in zip(col_tags, cols)])

    return cells, beside


def edge_kernel(helm, *rest):
    messages, (swap_b, swap_a) = rest[:-2], rest[-2:]
    rows, levels = helm.shape[0], (messages[0].shape[0] - 8) // HALF
    cells, beside = unpack(messages, levels)
    lane8 = lane_ids(8)

    def message(edge, beyond):
        x, out = cells(edge), beside(edge)
        image = across(helm[edge : edge + 1, :], x, out) - cells(beyond)
        corner = out[:8]
        for g in range(1, levels // 8):
            turned = pltpu.roll(out[8 * g : 8 * g + 8], 2 * g, 1)
            corner = jnp.where((lane8 == 2 * g - 1) | (lane8 == 2 * g), turned, corner)
        return x, image, corner

    low, high = message(0, 1), message(rows - 1, rows - 2)
    even = lax.rem(lax.axis_index("dom"), 2) == 0
    at = 0
    for a, b in zip(low, high):
        to = pl.ds(at, a.shape[0])
        swap_a[to] = jnp.where(even, b, a)
        swap_b[to] = jnp.where(even, a, b)
        at += a.shape[0]


def inner_kernel(groups, helm, *rest):
    messages, (field, image, second, sums, outer, helm_outer) = rest[:groups], rest[groups:]
    rows, levels = helm.shape[0], sums.shape[0] // 4
    pitch = rows + PAD
    me, comps = lax.axis_index("comp"), lax.axis_size("comp")
    lane, lane8 = lane_ids(levels), lane_ids(8)
    field[...] = jnp.zeros_like(field)
    outer[...] = jnp.zeros_like(outer)
    helm_outer[...] = jnp.zeros_like(helm_outer)
    low, high = lane < 2, lane >= LANES - 2
    for step, got in zip(steps_of(groups), messages):
        side, ends = side_of(got, levels)

        def row_of(j):
            label = side[0:1, LABEL + j : LABEL + j + 1].astype(jnp.int32)[0, 0]
            return pl.ds(PAD + lax.max(label, 0), levels, stride=pitch)

        turned = (pltpu.roll(ends, LANES - 2, 1), pltpu.roll(ends, 2, 1))
        for j in range(HALF):
            field[row_of(j), :] += got[j * levels : (j + 1) * levels]
            outer[row_of(HALF + j), :] += jnp.where(high, turned[1] if j else ends, 0.0)
            outer[row_of(2 * HALF + j), :] += jnp.where(low, turned[0] if j else ends, 0.0)
        if step:
            _, source = peer_of(me, step, groups)
            mine = ((lane8 == LANES - 1) & (source == me - 1)) | ((lane8 == 0) & (source == me + 1))
            for g in range(rows // 8):
                at = pl.ds(8 * g, 8)
                helm_outer[at, :] = jnp.where(
                    mine, pltpu.roll(side, LANES - (HELM + 2 * g + 1), 1), helm_outer[at, :]
                )
    inside = ((lane8 == LANES - 1) & (me > 0)) | ((lane8 == 0) & (me < comps - 1))
    sub = lax.broadcasted_iota(jnp.int32, (8, LANES), 0)
    for n in range(levels + 1):
        image[pl.ds(n * pitch, PAD), :] = jnp.zeros((PAD, LANES), jnp.float32)

    def beside(ref, at):
        return ref[pl.ds(at - 1, 8), :] + ref[pl.ds(at + 1, 8), :]

    def off_rim(x, g, width):
        if g == 0:
            x = jnp.where(sub < width, 0.0, x)
        if g == rows // 8 - 1:
            x = jnp.where(sub >= 8 - width, 0.0, x)
        return x

    for n in range(levels):
        at = [PAD + n * pitch + 8 * g for g in range(rows // 8)]
        xs = [field[pl.ds(a, 8), :] for a in at]
        es = [outer[pl.ds(a, 8), :] for a in at]
        us = [across(helm[8 * g : 8 * g + 8, :], xs[g], es[g]) - beside(field, a) for g, a in enumerate(at)]
        for a, u in zip(at, us):
            image[pl.ds(a, 8), :] = u
        parts = [[], [], [], []]
        for g, a in enumerate(at):
            x, e, u = xs[g], es[g], us[g]
            out = jnp.where(inside, across(helm_outer[8 * g : 8 * g + 8, :], e, x) - beside(outer, a), 0.0)
            z = across(helm[8 * g : 8 * g + 8, :], u, out) - beside(image, a)
            second[pl.ds(n * rows + 8 * g, 8), :] = z
            u1, u2 = off_rim(u, g, 1), off_rim(u, g, 2)
            for part, a, b in zip(parts, (x, x, u1, u2), (x, u1, u1, z)):
                part.append(a * b)
        for j, part in enumerate(parts):
            sums[pl.ds(j * levels + n, 1), :] = jnp.sum(total(part), axis=0, keepdims=True)


def rim_kernel(helm, field, image_in, second_in, sums, got_b, got_a, image, second, partial):
    rows, levels = helm.shape[0], sums.shape[0] // 4
    pitch = rows + PAD
    comp, comps = lax.axis_index("comp"), lax.axis_size("comp")
    dom, doms = lax.axis_index("dom"), lax.axis_size("dom")
    even = lax.rem(dom, 2) == 0
    lane = lane_ids(levels)
    inside = ((lane == LANES - 1) & (comp > 0)) | ((lane == 0) & (comp < comps - 1))
    parts = [sums[pl.ds(j * levels, levels), :] for j in range(4)]
    for side in range(2):
        from_b = even if side == 0 else jnp.logical_not(even)
        there = dom > 0 if side == 0 else dom < doms - 1
        first, second_row = (0, 1) if side == 0 else (rows - 1, rows - 2)
        at0, at1 = pl.ds(PAD + first, levels, stride=pitch), pl.ds(PAD + second_row, levels, stride=pitch)
        to0, to1 = pl.ds(first, levels, stride=rows), pl.ds(second_row, levels, stride=rows)

        def halo(start, size):
            at = pl.ds(start, size)
            return jnp.where(there, jnp.where(from_b, got_b[at], got_a[at]), 0.0)

        next_row, next_image, corner = halo(0, levels), halo(levels, levels), halo(2 * levels, 8)
        corners = [corner] + [pltpu.roll(corner, LANES - 2 * g, 1) for g in range(1, levels // 8)]
        next_outer = jnp.where(inside, jnp.concatenate(corners, axis=0), 0.0)
        r0, u1 = field[at0, :], image_in[at1, :]
        u0 = image_in[at0, :] - next_row
        beyond = next_image - jnp.where(there, r0, 0.0)
        h = helm[first : first + 1, :]
        z0 = second_in[to0, :] - (across(h, next_row, next_outer) + beyond)
        z1 = second_in[to1, :] + next_row
        image[at0, :] = u0
        second[to0, :] = z0
        second[to1, :] = z1
        parts[1] = parts[1] + r0 * u0
        parts[2] = parts[2] + u0 * u0
        parts[3] = parts[3] + (u0 * z0 + u1 * z1)
    stacked = jnp.concatenate(parts + [jnp.zeros((LANES - 4 * levels, LANES), jnp.float32)], axis=0)
    line = jnp.sum(stacked.T, axis=0, keepdims=True)
    for d in range(partial.shape[0]):
        partial[d] = line


def final_kernel(partials, field, image, second, solution_out, residual_out, solution, residual, sems):
    levels, rows = residual_out.shape[0], residual_out.shape[1]
    line = total([partials[d] for d in range(partials.shape[0])])
    lane = lane_ids(levels)
    level = lax.broadcasted_iota(jnp.int32, (levels, LANES), 0)
    rr, p, q, s = [
        jnp.sum(jnp.where(lane == level + j * levels, line, 0.0), axis=1, keepdims=True) for j in range(4)
    ]
    mean = p / rr
    square = q / rr
    spread = square - mean * mean
    third = s / rr - mean * (3.0 * square - 2.0 * mean * mean)
    along = SHIFT + mean
    a0 = 1.0 / along
    beta = a0 * a0 * spread
    a1 = 1.0 / (third / spread + along - a0 * spread)
    c1 = 1.0 + beta - SHIFT * a0
    coefs = (
        a0 + a1 * c1,
        -a1 * a0,
        1.0 - SHIFT * a0 - SHIFT * a1 * c1,
        -a0 - a1 * (c1 - SHIFT * a0),
        a1 * a0,
    )
    coefs = [jnp.broadcast_to(c, (levels, LANES)) for c in coefs]
    copies = []
    for n in range(levels):
        sol_r, sol_u, res_r, res_u, res_z = [jnp.broadcast_to(c[n : n + 1], (8, LANES)) for c in coefs]
        for g in range(rows // 8):
            at, to = pl.ds(PAD + n * (rows + PAD) + 8 * g, 8), pl.ds(8 * g, 8)
            x, u, z = field[at, :], image[at, :], second[pl.ds(n * rows + 8 * g, 8), :]
            solution[n, to, :] = sol_r * x + sol_u * u
            residual[n, to, :] = (res_r * x + res_u * u) + res_z * z
        if (n + 1) % PART == 0:
            at = pl.ds(n + 1 - PART, PART)
            for src, dst in ((solution, solution_out), (residual, residual_out)):
                copies.append(pltpu.make_async_copy(src.at[at], dst.at[at], sems.at[len(copies)]))
                copies[-1].start()
    for copy in copies:
        copy.wait()


def per_device(source_field, source_block, margin, remap_weight, helm):
    sources, weights = source_field[0, 0], remap_weight[0, 0]
    ids, marks = source_block[0, 0], margin[0, 0].T
    groups, doms = lax.axis_size("comp"), lax.axis_size("dom")
    levels = sources.shape[1]
    rows = helm.shape[0]
    f32 = lambda *shape: jax.ShapeDtypeStruct(shape, jnp.float32)
    slots = (groups + 2) * HALF
    messages = call(
        functools.partial(pack_kernel, groups),
        [f32(HALF * levels + 8, LANES)] * groups,
        [HBM] * 5,
        [
            pltpu.VMEM((slots, levels, LANES), jnp.float32),
            pltpu.SMEM((slots,), jnp.int32),
            pltpu.SMEM(ids.shape, jnp.int32),
            pltpu.SMEM(marks.shape, jnp.int32),
            pltpu.VMEM(sources.shape, sources.dtype),
            pltpu.VMEM(weights.shape, weights.dtype),
            pltpu.VMEM(helm.shape, helm.dtype),
            pltpu.SemaphoreType.DMA((4 + CHUNKS,)),
        ],
        name="pack",
    )(*[pltpu.with_memory_space_constraint(x, pltpu.HBM) for x in (ids, marks, sources, weights, helm)])
    arrived = [messages[0]]
    for step, message in list(zip(steps_of(groups), messages))[1:]:
        if groups & (groups - 1) == 0:
            pairs = [(c, c ^ step) for c in range(groups)]
        else:
            pairs = [(c, (c + step) % groups) for c in range(groups)]
        arrived.append(lax.ppermute(message, "comp", pairs))
    swap = f32(2 * levels + 8, LANES)
    swap_b, swap_a = call(edge_kernel, [swap, swap], [VMEM] * (1 + groups), name="edge")(helm, *arrived)

    def pairing(beside):
        pairs = []
        for c in range(groups):
            for d in range(doms):
                e = beside(d)
                there = (c, e) if 0 <= e < doms else (c ^ 1, d)
                if there[0] < groups:
                    pairs.append((c * doms + d, there[0] * doms + there[1]))
        return pairs

    got_b = lax.ppermute(swap_b, ("comp", "dom"), pairing(lambda d: ((d + 1) ^ 1) - 1))
    got_a = lax.ppermute(swap_a, ("comp", "dom"), pairing(lambda d: d ^ 1))
    flat, padded = f32(levels * rows, LANES), f32(PAD + levels * (rows + PAD), LANES)
    field, image, second, sums = call(
        functools.partial(inner_kernel, groups),
        [padded, padded, flat, f32(4 * levels, LANES)],
        [VMEM] * (1 + groups),
        [pltpu.VMEM(padded.shape, padded.dtype), pltpu.VMEM(helm.shape, helm.dtype)],
        name="inner",
        flops=60 * rows * levels * LANES,
    )(helm, *arrived)
    image, second, partial = call(
        rim_kernel,
        [padded, flat, f32(groups * doms, 1, LANES)],
        [VMEM] * 7,
        name="rim",
        aliases={2: 0, 3: 1},
    )(helm, field, image, second, sums, got_b, got_a)
    partials = lax.all_to_all(partial, ("comp", "dom"), split_axis=0, concat_axis=0, tiled=True)
    whole = f32(levels, rows, LANES)
    return tuple(
        call(
            final_kernel,
            [whole, whole],
            [VMEM] * 4,
            [pltpu.VMEM(whole.shape, whole.dtype)] * 2 + [pltpu.SemaphoreType.DMA((2 * levels // PART,))],
            name="final",
            out_spec=HBM,
        )(partials, field, image, second)
    )


def solution(mesh):
    placed = (
        P("comp", "dom", None, None, None),
        P("comp", "dom", None),
        P("comp", "dom", None, None),
        P("comp", "dom", None, None, None),
        P("dom", "comp"),
    )
    return jax.shard_map(
        per_device,
        mesh=mesh,
        in_specs=placed,
        out_specs=(P(None, "dom", "comp"), P(None, "dom", "comp")),
        check_vma=False,
    )
```

```python
import functools
import jax
import jax.numpy as jnp
from jax import lax
from jax.experimental import pallas as pl
from jax.experimental.pallas import tpu as pltpu
from jax.sharding import PartitionSpec as P

HALF = 2
LANES = 128
LABEL = 8
APART = 32
HELM = 16
SHIFT = 4.0
PART = 8
PAD = 8
CHUNKS = 1

VMEM = pl.BlockSpec(memory_space=pltpu.VMEM)
HBM = pl.BlockSpec(memory_space=pltpu.HBM)


def call(kernel, out_shape, in_specs, scratch=(), name=None, out_spec=VMEM, flops=0, aliases={}):
    return pl.pallas_call(
        kernel,
        out_shape=out_shape,
        in_specs=in_specs,
        out_specs=jax.tree.map(lambda _: out_spec, out_shape),
        scratch_shapes=scratch,
        input_output_aliases=aliases,
        name=name,
        compiler_params=pltpu.CompilerParams(vmem_limit_bytes=16 * 1024 * 1024),
        cost_estimate=pl.CostEstimate(flops=flops, bytes_accessed=flops // 8, transcendentals=0) if flops else None,
    )


def peer_of(me, step, devices):
    if devices & (devices - 1) == 0:
        return me ^ step, me ^ step
    return lax.rem(me + step, devices), lax.rem(me + devices - step, devices)


def steps_of(devices):
    return [*range(0, devices, 2), *range(1, devices, 2)]


def lane_ids(rows):
    return lax.broadcasted_iota(jnp.int32, (rows, LANES), 1)


def left(x, beside):
    return pltpu.roll(jnp.where(lane_ids(x.shape[0]) == LANES - 1, beside, x), 1, 1)


def right(x, beside):
    return pltpu.roll(jnp.where(lane_ids(x.shape[0]) == 0, beside, x), LANES - 1, 1)


def across(h, x, beside):
    return h * x - (left(x, beside) + right(x, beside))


def total(parts):
    while len(parts) > 1:
        parts = [a + b for a, b in zip(parts[::2], parts[1::2])] + parts[len(parts) // 2 * 2 :]
    return parts[0]


def pack_kernel(groups, ids_in, margin_in, sources_in, weights_in, helm_in, *rest):
    messages = rest[:groups]
    slots, labels, ids, margin, sources, weights, helm, sems = rest[groups:]
    levels = sources.shape[1]
    entries = ids.shape[0]
    copies = [
        pltpu.make_async_copy(src, dst, sems.at[j])
        for j, (src, dst) in enumerate(((margin_in, margin), (ids_in, ids), (sources_in, sources), (helm_in, helm)))
    ]
    cuts = [entries * j // CHUNKS for j in range(CHUNKS + 1)]
    chunks = []
    for j, (lo, hi) in enumerate(zip(cuts, cuts[1:])):
        at = pl.ds(lo, hi - lo)
        chunks.append(pltpu.make_async_copy(weights_in.at[at], weights.at[at], sems.at[len(copies) + j]))
    for copy in copies[:2] + chunks + copies[2:]:
        copy.start()
    slots[...] = jnp.zeros_like(slots)
    for at in range((groups + 2) * HALF):
        labels[at] = -1
    me = lax.axis_index("comp")
    lane = lane_ids(levels)
    lane8 = lane_ids(8)
    bases = [(peer_of(me, step, groups)[0] + 1) * HALF for step in steps_of(groups)]
    copies[0].wait()
    places = []
    for k in range(entries):
        base = (margin[0, k] + 1) * HALF
        row = margin[1, k]
        first = labels[base]
        later = jnp.logical_and(first >= 0, first != row).astype(jnp.int32)
        labels[base + later] = row
        places.append(base + later)
    copies[3].wait()
    packed = jnp.zeros((8, LANES), jnp.float32)
    for g in range(helm.shape[0] // 8):
        at = HELM + 2 * g
        turned = pltpu.roll(helm[8 * g : 8 * g + 8, :], at + 1, 1)
        packed = jnp.where((lane8 == at) | (lane8 == at + 1), turned, packed)
    for base, out in zip(bases, messages):
        side = packed
        for j in range(3 * HALF):
            at = base + (j % HALF) + (0, -HALF, HALF)[j // HALF]
            side = jnp.where(lane8 == LABEL + j, labels[at].astype(jnp.float32), side)
        out[HALF * levels :] = side
    copies[1].wait()
    copies[2].wait()
    for chunk in chunks:
        chunk.wait()
    parts = [
        lax.dot_general(sources[ids[k]], weights[k], (((1,), (1,)), ((), ())), preferred_element_type=jnp.float32)
        for k in range(entries)
    ]
    for k in range(entries):
        slots[places[k]] += parts[k]
    for base, out in zip(bases, messages):
        out[0:levels] = slots[base]
        out[levels : 2 * levels] = slots[base + 1]
        before, after = base - HALF, base + HALF
        cols = jnp.where(lane < LANES // 2, slots[after], slots[before])
        inner = jnp.where(
            lane < LANES // 2, pltpu.roll(slots[after + 1], 2, 1), pltpu.roll(slots[before + 1], LANES - 2, 1)
        )
        cols = jnp.where((lane < 2) | (lane >= LANES - 2), cols, inner)
        side = out[HALF * levels :]
        for g in range(levels // 8):
            turned = cols[8 * g : 8 * g + 8]
            if g:
                turned = pltpu.roll(turned, APART * g, 1)
            here = (lane8 + (LANES - APART * g + 4)) % LANES < 8
            side = jnp.where(here, turned, side)
        out[HALF * levels :] = side


def side_of(message, levels):
    side = message[HALF * levels :]
    turned = [side] + [pltpu.roll(side, LANES - APART * g, 1) for g in range(1, levels // 8)]
    return side, jnp.concatenate(turned, axis=0)


def unpack(messages, levels):
    lane = lane_ids(levels)
    blocks, tags, cols, col_tags = [], [], [], []
    for got in messages:
        side, ends = side_of(got, levels)
        tag = lambda j: jnp.broadcast_to(side[0:1, LABEL + j : LABEL + j + 1], (levels, LANES))
        blocks += [got[0:levels], got[levels : 2 * levels]]
        tags += [tag(0), tag(1)]
        inner = jnp.where(lane < LANES // 2, pltpu.roll(ends, LANES - 2, 1), pltpu.roll(ends, 2, 1))
        cols += [ends, inner]
        col_tags += [jnp.where(lane < LANES // 2, tag(4), tag(2)), jnp.where(lane < LANES // 2, tag(5), tag(3))]

    def cells(row):
        return total([jnp.where(t == float(row), b, 0.0) for t, b in zip(tags, blocks)])

    def beside(row):
        return total([jnp.where(t == float(row), b, 0.0) for t, b in zip(col_tags, cols)])

    return cells, beside


def edge_kernel(helm, *rest):
    messages, (swap_b, swap_a) = rest[:-2], rest[-2:]
    rows, levels = helm.shape[0], (messages[0].shape[0] - 8) // HALF
    cells, beside = unpack(messages, levels)
    lane = lane_ids(levels)

    def message(edge, beyond):
        x, out = cells(edge), beside(edge)
        lo, hi = left(x, out), right(x, out)
        corner = jnp.where(lane == 0, lo, jnp.where(lane == LANES - 1, hi, 0.0))
        return x, helm[edge : edge + 1, :] * x - ((lo + hi) + (cells(beyond) + corner))

    low, high = message(0, 1), message(rows - 1, rows - 2)
    even = lax.rem(lax.axis_index("dom"), 2) == 0
    at = 0
    for a, b in zip(low, high):
        to = pl.ds(at, a.shape[0])
        swap_a[to] = jnp.where(even, b, a)
        swap_b[to] = jnp.where(even, a, b)
        at += a.shape[0]


def inner_kernel(groups, helm, *rest):
    messages, (field, image, second, sums, outer, helm_outer) = rest[:groups], rest[groups:]
    rows, levels = helm.shape[0], sums.shape[0] // 4
    pitch = rows + PAD
    me, comps = lax.axis_index("comp"), lax.axis_size("comp")
    lane, lane8 = lane_ids(levels), lane_ids(8)
    field[...] = jnp.zeros_like(field)
    outer[...] = jnp.zeros_like(outer)
    helm_outer[...] = jnp.zeros_like(helm_outer)
    low, high = lane < 2, lane >= LANES - 2
    for step, got in zip(steps_of(groups), messages):
        side, ends = side_of(got, levels)

        def row_of(j):
            label = side[0:1, LABEL + j : LABEL + j + 1].astype(jnp.int32)[0, 0]
            return pl.ds(PAD + lax.max(label, 0), levels, stride=pitch)

        turned = (pltpu.roll(ends, LANES - 2, 1), pltpu.roll(ends, 2, 1))
        for j in range(HALF):
            field[row_of(j), :] += got[j * levels : (j + 1) * levels]
            outer[row_of(HALF + j), :] += jnp.where(high, turned[1] if j else ends, 0.0)
            outer[row_of(2 * HALF + j), :] += jnp.where(low, turned[0] if j else ends, 0.0)
        if step:
            _, source = peer_of(me, step, groups)
            mine = ((lane8 == LANES - 1) & (source == me - 1)) | ((lane8 == 0) & (source == me + 1))
            for g in range(rows // 8):
                at = pl.ds(8 * g, 8)
                helm_outer[at, :] = jnp.where(
                    mine, pltpu.roll(side, LANES - (HELM + 2 * g + 1), 1), helm_outer[at, :]
                )
    inside = ((lane8 == LANES - 1) & (me > 0)) | ((lane8 == 0) & (me < comps - 1))
    sub = lax.broadcasted_iota(jnp.int32, (8, LANES), 0)
    for n in range(levels + 1):
        image[pl.ds(n * pitch, PAD), :] = jnp.zeros((PAD, LANES), jnp.float32)

    def beside(ref, at):
        return ref[pl.ds(at - 1, 8), :] + ref[pl.ds(at + 1, 8), :]

    def off_rim(x, g, width):
        if g == 0:
            x = jnp.where(sub < width, 0.0, x)
        if g == rows // 8 - 1:
            x = jnp.where(sub >= 8 - width, 0.0, x)
        return x

    for n in range(levels):
        at = [PAD + n * pitch + 8 * g for g in range(rows // 8)]
        xs = [field[pl.ds(a, 8), :] for a in at]
        es = [outer[pl.ds(a, 8), :] for a in at]
        us = [across(helm[8 * g : 8 * g + 8, :], xs[g], es[g]) - beside(field, a) for g, a in enumerate(at)]
        for a, u in zip(at, us):
            image[pl.ds(a, 8), :] = u
        parts = [[], [], [], []]
        for g, a in enumerate(at):
            x, e, u = xs[g], es[g], us[g]
            out = jnp.where(inside, across(helm_outer[8 * g : 8 * g + 8, :], e, x) - beside(outer, a), 0.0)
            z = across(helm[8 * g : 8 * g + 8, :], u, out) - beside(image, a)
            second[pl.ds(n * rows + 8 * g, 8), :] = z
            u1, u2 = off_rim(u, g, 1), off_rim(u, g, 2)
            for part, a, b in zip(parts, (x, x, u1, u2), (x, u1, u1, z)):
                part.append(a * b)
        for j, part in enumerate(parts):
            sums[pl.ds(j * levels + n, 1), :] = jnp.sum(total(part), axis=0, keepdims=True)


def rim_kernel(helm, field, image_in, second_in, sums, got_b, got_a, image, second, partial):
    rows, levels = helm.shape[0], sums.shape[0] // 4
    pitch = rows + PAD
    dom, doms = lax.axis_index("dom"), lax.axis_size("dom")
    even = lax.rem(dom, 2) == 0
    parts = [sums[pl.ds(j * levels, levels), :] for j in range(4)]
    for side in range(2):
        from_b = even if side == 0 else jnp.logical_not(even)
        there = dom > 0 if side == 0 else dom < doms - 1
        first, second_row = (0, 1) if side == 0 else (rows - 1, rows - 2)
        at0, at1 = pl.ds(PAD + first, levels, stride=pitch), pl.ds(PAD + second_row, levels, stride=pitch)
        to0, to1 = pl.ds(first, levels, stride=rows), pl.ds(second_row, levels, stride=rows)

        def halo(start, size):
            at = pl.ds(start, size)
            return jnp.where(there, jnp.where(from_b, got_b[at], got_a[at]), 0.0)

        next_row, next_image = halo(0, levels), halo(levels, levels)
        r0, u1 = field[at0, :], image_in[at1, :]
        u0 = image_in[at0, :] - next_row
        beyond = next_image - jnp.where(there, r0, 0.0)
        h = helm[first : first + 1, :]
        z0 = second_in[to0, :] - (across(h, next_row, 0.0) + beyond)
        z1 = second_in[to1, :] + next_row
        image[at0, :] = u0
        second[to0, :] = z0
        second[to1, :] = z1
        parts[1] = parts[1] + r0 * u0
        parts[2] = parts[2] + u0 * u0
        parts[3] = parts[3] + (u0 * z0 + u1 * z1)
    stacked = jnp.concatenate(parts + [jnp.zeros((LANES - 4 * levels, LANES), jnp.float32)], axis=0)
    line = jnp.sum(stacked.T, axis=0, keepdims=True)
    for d in range(partial.shape[0]):
        partial[d] = line


def final_kernel(partials, field, image, second, solution_out, residual_out, solution, residual, sems):
    levels, rows = residual_out.shape[0], residual_out.shape[1]
    line = total([partials[d] for d in range(partials.shape[0])])
    lane = lane_ids(levels)
    level = lax.broadcasted_iota(jnp.int32, (levels, LANES), 0)
    rr, p, q, s = [
        jnp.sum(jnp.where(lane == level + j * levels, line, 0.0), axis=1, keepdims=True) for j in range(4)
    ]
    mean = p / rr
    square = q / rr
    spread = square - mean * mean
    third = s / rr - mean * (3.0 * square - 2.0 * mean * mean)
    along = SHIFT + mean
    a0 = 1.0 / along
    beta = a0 * a0 * spread
    a1 = 1.0 / (third / spread + along - a0 * spread)
    c1 = 1.0 + beta - SHIFT * a0
    coefs = (
        a0 + a1 * c1,
        -a1 * a0,
        1.0 - SHIFT * a0 - SHIFT * a1 * c1,
        -a0 - a1 * (c1 - SHIFT * a0),
        a1 * a0,
    )
    coefs = [jnp.broadcast_to(c, (levels, LANES)) for c in coefs]
    copies = []
    for n in range(levels):
        sol_r, sol_u, res_r, res_u, res_z = [jnp.broadcast_to(c[n : n + 1], (8, LANES)) for c in coefs]
        for g in range(rows // 8):
            at, to = pl.ds(PAD + n * (rows + PAD) + 8 * g, 8), pl.ds(8 * g, 8)
            x, u, z = field[at, :], image[at, :], second[pl.ds(n * rows + 8 * g, 8), :]
            solution[n, to, :] = sol_r * x + sol_u * u
            residual[n, to, :] = (res_r * x + res_u * u) + res_z * z
        if (n + 1) % PART == 0:
            at = pl.ds(n + 1 - PART, PART)
            for src, dst in ((solution, solution_out), (residual, residual_out)):
                copies.append(pltpu.make_async_copy(src.at[at], dst.at[at], sems.at[len(copies)]))
                copies[-1].start()
    for copy in copies:
        copy.wait()


def per_device(source_field, source_block, margin, remap_weight, helm):
    sources, weights = source_field[0, 0], remap_weight[0, 0]
    ids, marks = source_block[0, 0], margin[0, 0].T
    groups, doms = lax.axis_size("comp"), lax.axis_size("dom")
    levels = sources.shape[1]
    rows = helm.shape[0]
    f32 = lambda *shape: jax.ShapeDtypeStruct(shape, jnp.float32)
    slots = (groups + 2) * HALF
    messages = call(
        functools.partial(pack_kernel, groups),
        [f32(HALF * levels + 8, LANES)] * groups,
        [HBM] * 5,
        [
            pltpu.VMEM((slots, levels, LANES), jnp.float32),
            pltpu.SMEM((slots,), jnp.int32),
            pltpu.SMEM(ids.shape, jnp.int32),
            pltpu.SMEM(marks.shape, jnp.int32),
            pltpu.VMEM(sources.shape, sources.dtype),
            pltpu.VMEM(weights.shape, weights.dtype),
            pltpu.VMEM(helm.shape, helm.dtype),
            pltpu.SemaphoreType.DMA((4 + CHUNKS,)),
        ],
        name="pack",
    )(*[pltpu.with_memory_space_constraint(x, pltpu.HBM) for x in (ids, marks, sources, weights, helm)])
    arrived = [messages[0]]
    for step, message in list(zip(steps_of(groups), messages))[1:]:
        if groups & (groups - 1) == 0:
            pairs = [(c, c ^ step) for c in range(groups)]
        else:
            pairs = [(c, (c + step) % groups) for c in range(groups)]
        arrived.append(lax.ppermute(message, "comp", pairs))
    swap = f32(2 * levels, LANES)
    swap_b, swap_a = call(edge_kernel, [swap, swap], [VMEM] * (1 + groups), name="edge")(helm, *arrived)

    def pairing(beside):
        pairs = []
        for c in range(groups):
            for d in range(doms):
                e = beside(d)
                there = (c, e) if 0 <= e < doms else (c ^ 1, d)
                if there[0] < groups:
                    pairs.append((c * doms + d, there[0] * doms + there[1]))
        return pairs

    got_b = lax.ppermute(swap_b, ("comp", "dom"), pairing(lambda d: ((d + 1) ^ 1) - 1))
    got_a = lax.ppermute(swap_a, ("comp", "dom"), pairing(lambda d: d ^ 1))
    flat, padded = f32(levels * rows, LANES), f32(PAD + levels * (rows + PAD), LANES)
    field, image, second, sums = call(
        functools.partial(inner_kernel, groups),
        [padded, padded, flat, f32(4 * levels, LANES)],
        [VMEM] * (1 + groups),
        [pltpu.VMEM(padded.shape, padded.dtype), pltpu.VMEM(helm.shape, helm.dtype)],
        name="inner",
        flops=60 * rows * levels * LANES,
    )(helm, *arrived)
    image, second, partial = call(
        rim_kernel,
        [padded, flat, f32(groups * doms, 1, LANES)],
        [VMEM] * 7,
        name="rim",
        aliases={2: 0, 3: 1},
    )(helm, field, image, second, sums, got_b, got_a)
    partials = lax.all_to_all(partial, ("comp", "dom"), split_axis=0, concat_axis=0, tiled=True)
    whole = f32(levels, rows, LANES)
    return tuple(
        call(
            final_kernel,
            [whole, whole],
            [VMEM] * 4,
            [pltpu.VMEM(whole.shape, whole.dtype)] * 2 + [pltpu.SemaphoreType.DMA((2 * levels // PART,))],
            name="final",
            out_spec=HBM,
        )(partials, field, image, second)
    )


def solution(mesh):
    placed = (
        P("comp", "dom", None, None, None),
        P("comp", "dom", None),
        P("comp", "dom", None, None),
        P("comp", "dom", None, None, None),
        P("dom", "comp"),
    )
    return jax.shard_map(
        per_device,
        mesh=mesh,
        in_specs=placed,
        out_specs=(P(None, "dom", "comp"), P(None, "dom", "comp")),
        check_vma=False,
    )
```
